256 devices in a mesh: lat: 16 (over y_hi, z), lon: 16 (over x, y_lo, core).
Axes of the slice: x: 4, y: 4 (y_hi: 2, y_lo: 2; y = y_hi * 2 + y_lo), z: 8, core: 2. Of those that a mesh axis runs over, the one named last changes fastest.
Arguments:
- query_tok: bfloat16 [256, 1024, 512], P('lat', 'lon'), may hold values from -6 to 6
- key_tok: bfloat16 [256, 1024, 512], P('lat', 'lon'), may hold values from -6 to 6
- value_tok: bfloat16 [256, 1024, 512], P('lat', 'lon'), may hold values from -6 to 6
- output_tok: bfloat16 [256, 1024, 512], P('lat', 'lon'), may hold values from -6 to 6
- grad_output: bfloat16 [256, 1024, 512], P('lat', 'lon'), may hold values from -6 to 6
- log_totals: float32 [8, 256, 1024], P(None, 'lat', 'lon'), may hold values from 2 to 4
Outputs:
- grad_query: bfloat16 [256, 1024, 512], P('lat', 'lon')
- grad_key: bfloat16 [256, 1024, 512], P('lat', 'lon')
- grad_value: bfloat16 [256, 1024, 512], P('lat', 'lon')
The draws below stay inside these ranges and needn't reach their ends.
All inputs are finite; a program needn't handle non-finite values.
Results may differ from the reference program's by a relative error of at most 0.0053.
Values may be sent and summed in bfloat16 or wider, within the bound.
A program may use at most 64 MiB of HBM per device.

```python
import jax
import jax.numpy as jnp
from jax import lax

HEADS = 8
HEAD_DIM = 64
WIDTH = 512
NLAT = 256
NLON = 1024


def steps_of(rng, extent, shards, low, high):
    def one(position, blocks):
        heights = jax.random.uniform(jax.random.fold_in(jax.random.fold_in(rng, 6), position), (blocks,), jnp.float32, low / len(shards), high / len(shards))
        return jnp.repeat(jnp.exp(heights), extent[position] // blocks).reshape((-1,) + (1,) * (len(extent) - position - 1))

    level = one(*shards[0])
    for cut in shards[1:]:
        level = level * one(*cut)
    return level


def bell_draw(stream_key, dims, width, limit, split=(), held_as=jnp.bfloat16):
    gain = steps_of(stream_key, dims, split, -0.22, 0.18) if split else 1.0
    values = jax.random.normal(stream_key, dims, jnp.float32) * width * gain
    return jnp.minimum(jnp.maximum(values, -limit), limit).astype(held_as)


def setup_inputs(seed: int = 0) -> dict:
    key_list = jax.random.split(jax.random.key(seed), 7)
    return {
        "query_tok": bell_draw(key_list[0], (NLAT, NLON, WIDTH), 1.0, 6.0, ((0, 16), (1, 16))),
        "key_tok": bell_draw(key_list[1], (NLAT, NLON, WIDTH), 1.0, 6.0, ((0, 16), (1, 16))),
        "value_tok": bell_draw(key_list[2], (NLAT, NLON, WIDTH), 1.0, 6.0, ((0, 16), (1, 16))),
        "output_tok": bell_draw(key_list[3], (NLAT, NLON, WIDTH), 1.0, 6.0, ((0, 16), (1, 16))),
        "grad_output": bell_draw(key_list[4], (NLAT, NLON, WIDTH), 1.0, 6.0, ((0, 16), (1, 16))),
        "log_totals": jnp.clip(2.0 + 2.0 * jax.random.uniform(key_list[5], (HEADS, NLAT, NLON), jnp.float32) ** steps_of(key_list[5], (HEADS, NLAT, NLON), ((1, 16), (2, 16)), -0.2, 0.2), 2.0, 4.0),
    }


def reference(query_tok, key_tok, value_tok, output_tok, grad_output, log_totals):
    factor = HEAD_DIM ** -0.5
    grid_shape = (NLAT, NLON, HEADS, HEAD_DIM)
    queries = query_tok.astype(jnp.float32).reshape(grid_shape)
    keys_all = key_tok.astype(jnp.float32).reshape(grid_shape)
    values_all = value_tok.astype(jnp.float32).reshape(grid_shape)
    outputs = output_tok.astype(jnp.float32).reshape(grid_shape)
    grads = grad_output.astype(jnp.float32).reshape(grid_shape)
    delta = jnp.sum(grads * outputs, axis=-1)
    totals = jnp.transpose(log_totals, (1, 2, 0))
    rows_all = jnp.arange(NLAT, dtype=jnp.int32)
    first_row = jnp.clip(rows_all - 3, 0, NLAT - 7).astype(jnp.int32)
    cols_all = jnp.arange(NLON, dtype=jnp.int32)

    def visit(running, offset):
        grad_q, grad_k, grad_v = running
        row_step = offset // 7
        col_step = offset % 7 - 3
        key_rows = (first_row + row_step).astype(jnp.int32)
        key_cols = ((cols_all + col_step) % NLON).astype(jnp.int32)
        window_keys = keys_all[key_rows][:, key_cols]
        window_values = values_all[key_rows][:, key_cols]
        scores = jnp.sum(queries * window_keys, axis=-1) * factor
        weights = jnp.exp(scores - totals)
        weights_low = lax.optimization_barrier(weights.astype(jnp.bfloat16)).astype(jnp.float32)
        prob_grad = jnp.sum(grads * window_values, axis=-1)
        score_grad = lax.optimization_barrier((weights * (prob_grad - delta)).astype(jnp.bfloat16)).astype(jnp.float32)
        grad_q = grad_q + score_grad[..., None] * window_keys
        grad_k = grad_k.at[key_rows[:, None], key_cols[None, :]].add(score_grad[..., None] * queries)
        grad_v = grad_v.at[key_rows[:, None], key_cols[None, :]].add(weights_low[..., None] * grads)
        return (grad_q, grad_k, grad_v), None

    zeros = jnp.zeros(grid_shape, jnp.float32)
    (grad_q, grad_k, grad_v), _ = lax.scan(visit, (zeros, zeros, zeros), jnp.arange(49, dtype=jnp.int32))
    flat_shape = (NLAT, NLON, HEADS * HEAD_DIM)
    return ((grad_q * factor).reshape(flat_shape).astype(jnp.bfloat16),
            (grad_k * factor).reshape(flat_shape).astype(jnp.bfloat16),
            grad_v.reshape(flat_shape).astype(jnp.bfloat16))
```

```python
import functools

import jax
import jax.numpy as jnp
from jax import lax
from jax.experimental import pallas as pl
from jax.experimental.pallas import tpu as pltpu
from jax.sharding import PartitionSpec as P

MESH = pl.DeviceIdType.MESH
BF = jnp.bfloat16
F32 = jnp.float32
BIG = 32768.0
EXP_SCALE = 0.125 * 1.4426950408889634
CHUNKS = 2


def _iota(shape, dim):
    return lax.broadcasted_iota(jnp.int32, shape, dim)


def _dot(a, b, dims):
    return lax.dot_general(a, b, (dims, ((), ())), preferred_element_type=F32)


def _keep(mask, x):
    return jnp.where(mask, x, jnp.zeros_like(x))


def _flat(x):
    return x.reshape(-1, x.shape[-1])


def _key_features(base, row0, rows, q_base, total):
    shape = (2 * rows * 8, 128)
    key = _iota(shape, 0)
    lane = _iota(shape, 1)
    tile = key // (rows * 8)
    k_row = base + row0 + key // 8 % rows
    k_col = tile * 8 + key % 8
    group, slot = lane // 16, lane % 16
    q_row = q_base + 2 * group + slot - 6
    first = jnp.clip(q_row - 3, 0, total - 7)
    row_ok = (k_row >= first) & (k_row < first + 7)
    gap = k_col - 4 - group
    col_ok = (gap >= -3) & (gap <= 3)
    row_slot = (slot == 6) | (slot == 7)
    bad = (row_slot & jnp.logical_not(row_ok)) | ((slot == 8) & jnp.logical_not(col_ok))
    value = jnp.where(bad, -BIG, jnp.where(slot < 3, -8.0, 0.0))
    return value.astype(BF)


def _prob_features(keys):
    slot = _iota((keys, 128), 1) % 16
    return jnp.where((slot >= 3) & (slot < 6), -1.0, 0.0).astype(BF)


def _split3(x):
    a = x.astype(BF).astype(F32)
    rest = x - a
    b = rest.astype(BF).astype(F32)
    return a, b, rest - b


def kernel(
    n_lat,
    n_lon,
    q_hbm,
    k_hbm,
    v_hbm,
    o_hbm,
    g_hbm,
    lt_hbm,
    dq_out,
    dk_out,
    dv_out,
    qv,
    kv,
    vv,
    ov,
    gv,
    ltv,
    aug,
    ksh,
    vsh,
    dq_acc,
    dk_acc,
    dv_acc,
    feat,
    feat_halo,
    rim_in,
    q_halo,
    g_halo,
    a_halo,
    dq_send,
    dq_recv,
    rim_send,
    rim_recv,
    load_sem,
    rim_sems,
    row_sems,
    back_sems,
    grad_sems,
):
    lat = lax.axis_index("lat")
    lon = lax.axis_index("lon")
    left = (lat, lax.rem(lon + n_lon - 1, n_lon))
    right = (lat, lax.rem(lon + 1, n_lon))
    above = (lat - 1, lon)
    below = (lat + 1, lon)
    has_above = lat > 0
    has_below = lat < n_lat - 1
    total = n_lat * 16
    base = lat * 16
    width = 8 // CHUNKS

    loads = [
        pltpu.make_async_copy(src, dst, load_sem.at[i])
        for i, (src, dst) in enumerate(
            ((g_hbm, gv), (o_hbm, ov), (lt_hbm, ltv), (k_hbm, kv), (v_hbm, vv), (q_hbm, qv))
        )
    ]
    for load in loads:
        load.start()

    barrier = pltpu.get_barrier_semaphore()

    def greet(device):
        pl.semaphore_signal(barrier, inc=1, device_id=device, device_id_type=MESH)

    greet(left)
    greet(right)
    pl.when(has_above)(lambda: greet(above))
    pl.when(has_below)(lambda: greet(below))
    peers = 2 + jnp.minimum(lat, 1) + jnp.minimum(n_lat - 1 - lat, 1)
    pl.semaphore_wait(barrier, peers)

    def remote(src, dst, sems, index, device):
        return pltpu.make_async_remote_copy(
            src_ref=src,
            dst_ref=dst,
            send_sem=sems.at[(0,) + index],
            recv_sem=sems.at[(1,) + index],
            device_id=device,
            device_id_type=MESH,
        )

    def row_copy(what, chunk, side):
        src, dst = ((q_hbm, q_halo), (g_hbm, g_halo), (aug, a_halo))[what]
        rows = pl.ds(13, 3) if side == 0 else pl.ds(0, 3)
        strips = pl.ds(chunk * width, width)
        return remote(
            src.at[rows, strips],
            dst.at[side, pl.ds(0, 3), strips],
            row_sems,
            (what, chunk, side),
            below if side == 0 else above,
        )

    def rim_copy(what, side):
        src = (k_hbm, v_hbm)[what]
        return remote(
            src.at[:, 7 if side == 0 else 0],
            rim_in.at[side, what],
            rim_sems,
            (what, side),
            right if side == 0 else left,
        )

    def back_copy(chunk, side):
        strips = pl.ds(chunk * width, width)
        return remote(
            dq_send.at[side, :, strips],
            dq_recv.at[1 - side, :, strips],
            back_sems,
            (chunk, 1 - side),
            above if side == 0 else below,
        )

    def grad_copy(what, side):
        return remote(
            rim_send.at[side, what],
            rim_recv.at[side, what],
            grad_sems,
            (what, side),
            right if side == 0 else left,
        )

    def send_rows(whats, side):
        for chunk in range(CHUNKS):
            for what in whats:
                row_copy(what, chunk, side).start()

    pl.when(has_below)(lambda: send_rows((0, 1), 0))
    pl.when(has_above)(lambda: send_rows((0, 1), 1))
    for what in range(2):
        for side in range(2):
            rim_copy(what, side).start()

    slot16 = _iota((1, 128), 1) % 16
    group16 = _iota((1, 128), 1) // 16
    low = _iota((1, 128), 1) < 64
    head_keep = [(group16 == h) | (slot16 >= 6) for h in range(8)]
    for t in range(2):
        feat[t] = _key_features(base, 8 * t, 8, base, total)
    feat_halo[0] = _key_features(base, 0, 4, base - 16, total)
    feat_halo[1] = _key_features(base, 12, 4, base + 16, total)

    @pl.loop(0, 9)
    def _(tile):
        dk_acc[tile] = jnp.zeros((16, 8, 512), F32)
        dv_acc[tile] = jnp.zeros((16, 8, 512), F32)

    for side in range(2):
        q_halo[side, 3] = jnp.zeros((8, 8, 512), BF)
        g_halo[side, 3] = jnp.zeros((8, 8, 512), BF)
        a_halo[side, 3] = jnp.zeros((8, 8, 128), BF)

    feature = _iota((512, 128), 0)
    lane = _iota((512, 128), 1)
    spread = jnp.where(
        (lane // 16 == feature // 64) & (lane % 16 >= 3) & (lane % 16 < 6), 1.0, 0.0
    ).astype(BF)
    for load in loads[:3]:
        load.wait()
    parts = _split3(ltv[...].T)
    column = _iota((64, 128), 0) % 8
    group = _iota((64, 128), 1) // 16
    slot = _iota((64, 128), 1) % 16
    col_hot = jnp.where((slot == 8) & (group == column), 1.0, 0.0)

    def features_of(r):
        product = _flat(gv[r].astype(F32)) * _flat(ov[r].astype(F32))
        high = product.astype(BF)
        rest = (product - high.astype(F32)).astype(BF)
        delta = _dot(high, spread, ((1,), (0,))) + _dot(rest, spread, ((1,), (0,)))
        d0, d1, d2 = _split3(delta)
        rolled = [pltpu.roll(part, (i - r) % 128, 1) for i, part in enumerate(parts)]
        value = jnp.where((slot >= 6) & (slot < 8) & (2 * group + slot - 6 == r), 1.0, col_hot)
        for i, x in enumerate(rolled + [d0, d1, d2]):
            value = jnp.where(slot == i, x, value)
        aug[r] = value.astype(BF).reshape(8, 8, 128)

    for r in (13, 14, 15):
        features_of(r)
    pl.when(has_below)(lambda: send_rows((2,), 0))
    for r in (0, 1, 2):
        features_of(r)
    pl.when(has_above)(lambda: send_rows((2,), 1))
    for r in range(3, 13):
        features_of(r)

    half = _iota((1, 8, 512), 1) < 4

    def turned(x):
        return pltpu.roll(x.astype(F32), 4, 1)

    for load in loads[3:5]:
        load.wait()

    @pl.loop(1, 8)
    def _(tile):
        for src, dst in ((kv, ksh), (vv, vsh)):
            dst[tile] = jnp.where(half, turned(src[:, tile - 1]), turned(src[:, tile])).astype(BF)

    loads[5].wait()
    prob_feat = _prob_features(128)

    def two(x):
        return jnp.concatenate([_keep(low, x), _keep(jnp.logical_not(low), x)], axis=0)

    def unit(s, t, p):
        lanes = pl.ds(128 * p, 128)
        k_rows = pl.ds(8 * t, 8)
        q_rows = pl.ds(4 * t, 12)
        keys = jnp.concatenate(
            [_flat(ksh[s, k_rows, :, lanes]), _flat(ksh[s + 1, k_rows, :, lanes])], axis=0
        )
        values = jnp.concatenate(
            [_flat(vsh[s, k_rows, :, lanes]), _flat(vsh[s + 1, k_rows, :, lanes])], axis=0
        )
        q2 = two(_flat(qv[q_rows, s, :, lanes]))
        g2 = two(_flat(gv[q_rows, s, :, lanes]))
        extra = _flat(aug[q_rows, s])
        a2 = jnp.concatenate(
            [_keep(head_keep[2 * p], extra), _keep(head_keep[2 * p + 1], extra)], axis=0
        )
        scores = _dot(
            jnp.concatenate([keys, feat[t]], axis=1),
            jnp.concatenate([q2, a2], axis=1),
            ((1,), (1,)),
        )
        prob_grad = _dot(
            jnp.concatenate([values, prob_feat], axis=1),
            jnp.concatenate([g2, a2], axis=1),
            ((1,), (1,)),
        )
        weights = jnp.exp2(scores * EXP_SCALE)
        score_grad = (weights * prob_grad).astype(BF)
        d_keys = _dot(score_grad, q2, ((1,), (0,)))
        d_values = _dot(weights.astype(BF), g2, ((1,), (0,)))
        turned_grad = score_grad.T
        d_query = _dot(
            jnp.concatenate([turned_grad[:96], turned_grad[96:]], axis=1),
            two(keys),
            ((1,), (0,)),
        )
        for acc, d in ((dk_acc, d_keys), (dv_acc, d_values)):
            acc[s, k_rows, :, lanes] += d[:64].reshape(8, 8, 128)
            acc[s + 1, k_rows, :, lanes] += d[64:].reshape(8, 8, 128)
        return d_query

    def strip(s):
        for p in range(4):
            lanes = pl.ds(128 * p, 128)
            upper = unit(s, 0, p)
            lower = unit(s, 1, p)
            dq_acc[pl.ds(0, 4), s, :, lanes] = upper[:32].reshape(4, 8, 128)
            dq_acc[pl.ds(4, 8), s, :, lanes] = (upper[32:] + lower[:64]).reshape(8, 8, 128)
            dq_acc[pl.ds(12, 4), s, :, lanes] = lower[64:].reshape(4, 8, 128)

    @pl.loop(1, 7)
    def _(s):
        strip(s)

    for what in range(2):
        for side in range(2):
            rim_copy(what, side).wait()
    for i, (src, dst) in enumerate(((kv, ksh), (vv, vsh))):
        dst[0] = jnp.where(half, turned(rim_in[0, i]), turned(src[:, 0])).astype(BF)
        dst[8] = jnp.where(half, turned(src[:, 7]), turned(rim_in[1, i])).astype(BF)

    @pl.loop(0, 2)
    def _(i):
        strip(7 * i)

    lane512 = _iota((1, 512), 1)
    prob_halo = _prob_features(64)

    def halo_unit(s, side):
        rows = pl.ds(12 * side, 4)
        keys = jnp.concatenate([_flat(ksh[s, rows]), _flat(ksh[s + 1, rows])], axis=0)
        values = jnp.concatenate([_flat(vsh[s, rows]), _flat(vsh[s + 1, rows])], axis=0)
        q = _flat(q_halo[side, :, s])
        g = _flat(g_halo[side, :, s])
        extra = _flat(a_halo[side, :, s])
        q8 = jnp.concatenate([_keep(lane512 // 64 == h, q) for h in range(8)], axis=0)
        g8 = jnp.concatenate([_keep(lane512 // 64 == h, g) for h in range(8)], axis=0)
        a8 = jnp.concatenate([_keep(head_keep[h], extra) for h in range(8)], axis=0)
        scores = _dot(
            jnp.concatenate([keys, feat_halo[side]], axis=1),
            jnp.concatenate([q8, a8], axis=1),
            ((1,), (1,)),
        )
        prob_grad = _dot(
            jnp.concatenate([values, prob_halo], axis=1),
            jnp.concatenate([g8, a8], axis=1),
            ((1,), (1,)),
        )
        weights = jnp.exp2(scores * EXP_SCALE)
        score_grad = (weights * prob_grad).astype(BF)
        d_keys = _dot(score_grad, q8, ((1,), (0,)))
        d_values = _dot(weights.astype(BF), g8, ((1,), (0,)))
        turned_grad = score_grad.T
        for p in range(4):
            lanes = slice(128 * p, 128 * p + 128)
            d_query = _dot(turned_grad[64 * p : 64 * p + 64], keys[:, lanes], ((1,), (0,)))
            d_query = jnp.where(low, d_query[:32], d_query[32:]) * 0.125
            dq_send[side, :, s, :, lanes] = d_query[:24].reshape(3, 8, 128).astype(BF)
        for acc, d in ((dk_acc, d_keys), (dv_acc, d_values)):
            acc[s, rows] += d[:32].reshape(4, 8, 512)
            acc[s + 1, rows] += d[32:].reshape(4, 8, 512)

    def halo(chunk, side):
        for what in range(3):
            row_copy(what, chunk, side).wait_recv()

        @pl.loop(chunk * width, (chunk + 1) * width)
        def _(s):
            halo_unit(s, side)

        back_copy(chunk, side).start()

    for chunk in range(CHUNKS):
        pl.when(has_above)(functools.partial(halo, chunk, 0))
        pl.when(has_below)(functools.partial(halo, chunk, 1))

    half8 = _iota((1, 8, 512), 1) < 4
    for what, acc in enumerate((dk_acc, dv_acc)):
        scale = 0.125 if what == 0 else 1.0
        for i in range(8):
            a, b = acc[8, 2 * i], acc[8, 2 * i + 1]
            rim_send[0, what, i] = (
                jnp.where(half8[0], pltpu.roll(a, 4, 0), b) * scale
            ).astype(BF)
            a, b = acc[0, 2 * i], acc[0, 2 * i + 1]
            rim_send[1, what, i] = (
                jnp.where(half8[0], a, pltpu.roll(b, 4, 0)) * scale
            ).astype(BF)
        for side in range(2):
            grad_copy(what, side).start()

    @pl.loop(3, 13)
    def _(r):
        dq_out[r] = (dq_acc[r] * 0.125).astype(BF)

    def merged(acc, j, scale):
        return pltpu.roll(jnp.where(half, acc[j + 1], acc[j]), 4, 1) * scale

    @pl.loop(1, 7)
    def _(j):
        dk_out[:, j] = merged(dk_acc, j, 0.125).astype(BF)
        dv_out[:, j] = merged(dv_acc, j, 1.0).astype(BF)

    for what in range(2):
        for side in range(2):
            grad_copy(what, side).wait()
    for what, (acc, out) in enumerate(((dk_acc, dk_out), (dv_acc, dv_out))):
        scale = 0.125 if what == 0 else 1.0
        edge = merged(acc, 0, scale)
        came = rim_recv[0, what].astype(F32)
        spun = pltpu.roll(came, 4, 1)
        for i in range(8):
            out[2 * i, 0] = (edge[2 * i] + _keep(half8[0], came[i])).astype(BF)
            out[2 * i + 1, 0] = (edge[2 * i + 1] + _keep(half8[0], spun[i])).astype(BF)
        edge = merged(acc, 7, scale)
        came = rim_recv[1, what].astype(F32)
        spun = pltpu.roll(came, 4, 1)
        for i in range(8):
            out[2 * i, 7] = (edge[2 * i] + _keep(jnp.logical_not(half8[0]), spun[i])).astype(BF)
            out[2 * i + 1, 7] = (
                edge[2 * i + 1] + _keep(jnp.logical_not(half8[0]), came[i])
            ).astype(BF)

    def finish(side, rows):
        @pl.when(has_above if side == 0 else has_below)
        def _():
            for chunk in range(CHUNKS):
                back_copy(chunk, 1 - side).wait_recv()
            for r in range(3):
                dq_out[rows + r] = (
                    dq_acc[rows + r] * 0.125 + dq_recv[side, r].astype(F32)
                ).astype(BF)

        @pl.when(jnp.logical_not(has_above if side == 0 else has_below))
        def _():
            for r in range(3):
                dq_out[rows + r] = (dq_acc[rows + r] * 0.125).astype(BF)

    finish(0, 0)
    finish(1, 13)

    def drain(send_side, back_side):
        for chunk in range(CHUNKS):
            for what in range(3):
                row_copy(what, chunk, send_side).wait_send()
            back_copy(chunk, back_side).wait_send()

    pl.when(has_below)(lambda: drain(0, 1))
    pl.when(has_above)(lambda: drain(1, 0))


def solution(mesh):
    n_lat, n_lon = mesh.shape["lat"], mesh.shape["lon"]

    def per_device(query_tok, key_tok, value_tok, output_tok, grad_output, log_totals):
        def tiled(x):
            return x.reshape(16, 8, 8, 512)

        dma = pltpu.SemaphoreType.DMA
        token = (16, 8, 8, 512)
        shifted = (9, 16, 8, 512)
        outs = pl.pallas_call(
            functools.partial(kernel, n_lat, n_lon),
            out_shape=[jax.ShapeDtypeStruct(token, BF)] * 3,
            in_specs=[pl.BlockSpec(memory_space=pl.ANY)] * 6,
            out_specs=[pl.BlockSpec(memory_space=pltpu.VMEM)] * 3,
            scratch_shapes=[
                pltpu.VMEM(token, BF),
                pltpu.VMEM(token, BF),
                pltpu.VMEM(token, BF),
                pltpu.VMEM(token, BF),
                pltpu.VMEM(token, BF),
                pltpu.VMEM((128, 64), F32),
                pltpu.VMEM((16, 8, 8, 128), BF),
                pltpu.VMEM(shifted, BF),
                pltpu.VMEM(shifted, BF),
                pltpu.VMEM(token, F32),
                pltpu.VMEM(shifted, F32),
                pltpu.VMEM(shifted, F32),
                pltpu.VMEM((2, 128, 128), BF),
                pltpu.VMEM((2, 64, 128), BF),
                pltpu.VMEM((2, 2, 16, 8, 512), BF),
                pltpu.VMEM((2, 4, 8, 8, 512), BF),
                pltpu.VMEM((2, 4, 8, 8, 512), BF),
                pltpu.VMEM((2, 4, 8, 8, 128), BF),
                pltpu.VMEM((2, 3, 8, 8, 512), BF),
                pltpu.VMEM((2, 3, 8, 8, 512), BF),
                pltpu.VMEM((2, 2, 8, 8, 512), BF),
                pltpu.VMEM((2, 2, 8, 8, 512), BF),
                dma((6,)),
                dma((2, 2, 2)),
                dma((2, 3, CHUNKS, 2)),
                dma((2, CHUNKS, 2)),
                dma((2, 2, 2)),
            ],
            compiler_params=pltpu.CompilerParams(
                collective_id=0,
                has_side_effects=True,
                vmem_limit_bytes=56 * 1024 * 1024,
            ),
        )(
            tiled(query_tok),
            tiled(key_tok),
            tiled(value_tok),
            tiled(output_tok),
            tiled(grad_output),
            log_totals.reshape(128, 64),
        )
        return tuple(x.reshape(16, 64, 512) for x in outs)

    return jax.shard_map(
        per_device,
        mesh=mesh,
        in_specs=(P("lat", "lon", None),) * 5 + (P(None, "lat", "lon"),),
        out_specs=(P("lat", "lon", None),) * 3,
        check_vma=False,
    )
```

```python
import functools

import jax
import jax.numpy as jnp
from jax import lax
from jax.experimental import pallas as pl
from jax.experimental.pallas import tpu as pltpu
from jax.sharding import PartitionSpec as P

MESH = pl.DeviceIdType.MESH
BF = jnp.bfloat16
F32 = jnp.float32
BIG = 32768.0
EXP_SCALE = 0.125 * 1.4426950408889634
CHUNKS = 2
LAG1 = 2
LAG2 = 2
PER = 2


def _iota(shape, dim):
    return lax.broadcasted_iota(jnp.int32, shape, dim)


def _dot(a, b, dims):
    return lax.dot_general(a, b, (dims, ((), ())), preferred_element_type=F32)


def _keep(mask, x):
    return jnp.where(mask, x, jnp.zeros_like(x))


def _flat(x):
    return x.reshape(-1, x.shape[-1])


def _key_features(base, row0, rows, q_base, total, tiles, spread):
    shape = (tiles * rows * 8, 128)
    key = _iota(shape, 0)
    lane = _iota(shape, 1)
    tile = key // (rows * 8)
    k_row = base + row0 + key // 8 % rows
    k_col = tile * 8 + key % 8
    group, slot = lane // 16, lane % 16
    q_row = q_base + 2 * group + slot - 6
    first = jnp.clip(q_row - 3, 0, total - 7)
    row_ok = (k_row >= first) & (k_row < first + 7)
    gap = k_col - 4 - group - jnp.where(slot == 9, spread, 0)
    col_ok = (gap >= -3) & (gap <= 3)
    row_slot = (slot == 6) | (slot == 7)
    bad = (row_slot & jnp.logical_not(row_ok)) | (
        ((slot == 8) | (slot == 9)) & jnp.logical_not(col_ok)
    )
    value = jnp.where(bad, -BIG, jnp.where(slot < 3, -8.0, 0.0))
    return value.astype(BF)


def _prob_features(keys):
    slot = _iota((keys, 128), 1) % 16
    return jnp.where((slot >= 3) & (slot < 6), -1.0, 0.0).astype(BF)


def _split3(x):
    a = x.astype(BF).astype(F32)
    rest = x - a
    b = rest.astype(BF).astype(F32)
    return a, b, rest - b


def kernel(
    n_lat,
    n_lon,
    q_hbm,
    k_hbm,
    v_hbm,
    o_hbm,
    g_hbm,
    lt_hbm,
    dq_out,
    dk_out,
    dv_out,
    qv,
    kv,
    vv,
    ov,
    gv,
    ltv,
    aug,
    ksh,
    vsh,
    dq_acc,
    dk_acc,
    dv_acc,
    feat,
    feat_halo,
    rim_in,
    q_halo,
    g_halo,
    a_halo,
    dq_send,
    dq_recv,
    rim_send,
    rim_recv,
    load_sem,
    rim_sems,
    row_sems,
    back_sems,
    grad_sems,
):
    lat = lax.axis_index("lat")
    lon = lax.axis_index("lon")
    left = (lat, lax.rem(lon + n_lon - 1, n_lon))
    right = (lat, lax.rem(lon + 1, n_lon))
    above = (lat - 1, lon)
    below = (lat + 1, lon)
    has_above = lat > 0
    has_below = lat < n_lat - 1
    total = n_lat * 16
    base = lat * 16
    width = 8 // CHUNKS

    loads = [
        pltpu.make_async_copy(src, dst, load_sem.at[i])
        for i, (src, dst) in enumerate(
            ((g_hbm, gv), (o_hbm, ov), (lt_hbm, ltv), (k_hbm, kv), (v_hbm, vv), (q_hbm, qv))
        )
    ]
    for load in loads:
        load.start()

    barrier = pltpu.get_barrier_semaphore()

    def greet(device):
        pl.semaphore_signal(barrier, inc=1, device_id=device, device_id_type=MESH)

    greet(left)
    greet(right)
    pl.when(has_above)(lambda: greet(above))
    pl.when(has_below)(lambda: greet(below))
    peers = 2 + jnp.minimum(lat, 1) + jnp.minimum(n_lat - 1 - lat, 1)
    pl.semaphore_wait(barrier, peers)

    def remote(src, dst, sems, index, device):
        return pltpu.make_async_remote_copy(
            src_ref=src,
            dst_ref=dst,
            send_sem=sems.at[(0,) + index],
            recv_sem=sems.at[(1,) + index],
            device_id=device,
            device_id_type=MESH,
        )

    def row_copy(what, chunk, side):
        src, dst = ((q_hbm, q_halo), (g_hbm, g_halo), (aug, a_halo))[what]
        rows = pl.ds(13, 3) if side == 0 else pl.ds(0, 3)
        strips = pl.ds(chunk * width, width)
        return remote(
            src.at[rows, strips],
            dst.at[side, pl.ds(0, 3), strips],
            row_sems,
            (what, chunk, side),
            below if side == 0 else above,
        )

    def rim_copy(what, side):
        src = (k_hbm, v_hbm)[what]
        return remote(
            src.at[:, 7 if side == 0 else 0],
            rim_in.at[side, what],
            rim_sems,
            (what, side),
            right if side == 0 else left,
        )

    def back_copy(chunk, side):
        strips = pl.ds(chunk * width, width)
        return remote(
            dq_send.at[side, :, strips],
            dq_recv.at[1 - side, :, strips],
            back_sems,
            (chunk, 1 - side),
            above if side == 0 else below,
        )

    def grad_copy(what, side):
        return remote(
            rim_send.at[side, what],
            rim_recv.at[side, what],
            grad_sems,
            (what, side),
            right if side == 0 else left,
        )

    def send_rows(whats, side):
        for chunk in range(CHUNKS):
            for what in whats:
                row_copy(what, chunk, side).start()

    pl.when(has_below)(lambda: send_rows((0, 1), 0))
    pl.when(has_above)(lambda: send_rows((0, 1), 1))
    for what in range(2):
        for side in range(2):
            rim_copy(what, side).start()

    slot16 = _iota((1, 128), 1) % 16
    group16 = _iota((1, 128), 1) // 16
    low = _iota((1, 128), 1) < 64
    head_keep = [(group16 == h) | (slot16 >= 6) for h in range(8)]
    for t in range(2):
        feat[t] = _key_features(base, 8 * t, 8, base, total, 2, 0)
    feat_halo[0] = _key_features(base, 0, 4, base - 16, total, 3, 8)
    feat_halo[1] = _key_features(base, 12, 4, base + 16, total, 3, 8)

    @pl.loop(0, 9)
    def _(tile):
        dk_acc[tile] = jnp.zeros((16, 8, 512), F32)
        dv_acc[tile] = jnp.zeros((16, 8, 512), F32)

    for side in range(2):
        q_halo[side, 3] = jnp.zeros((8, 8, 512), BF)
        g_halo[side, 3] = jnp.zeros((8, 8, 512), BF)
        a_halo[side, 3] = jnp.zeros((8, 8, 128), BF)

    feature = _iota((512, 128), 0)
    lane = _iota((512, 128), 1)
    spread = jnp.where(
        (lane // 16 == feature // 64) & (lane % 16 >= 3) & (lane % 16 < 6), 1.0, 0.0
    ).astype(BF)
    for load in loads[:3]:
        load.wait()
    parts = _split3(ltv[...].T)
    column = _iota((64, 128), 0) % 8
    group = _iota((64, 128), 1) // 16
    slot = _iota((64, 128), 1) % 16
    odd = _iota((64, 128), 0) // 8 % 2
    col_hot = jnp.where((slot == 8 + odd) & (group == column), 1.0, 0.0)

    def features_of(r):
        product = _flat(gv[r].astype(F32)) * _flat(ov[r].astype(F32))
        high = product.astype(BF)
        rest = (product - high.astype(F32)).astype(BF)
        delta = _dot(high, spread, ((1,), (0,))) + _dot(rest, spread, ((1,), (0,)))
        d0, d1, d2 = _split3(delta)
        rolled = [pltpu.roll(part, (i - r) % 128, 1) for i, part in enumerate(parts)]
        value = jnp.where((slot >= 6) & (slot < 8) & (2 * group + slot - 6 == r), 1.0, col_hot)
        for i, x in enumerate(rolled + [d0, d1, d2]):
            value = jnp.where(slot == i, x, value)
        aug[r] = value.astype(BF).reshape(8, 8, 128)

    for r in (13, 14, 15):
        features_of(r)
    pl.when(has_below)(lambda: send_rows((2,), 0))
    for r in (0, 1, 2):
        features_of(r)
    pl.when(has_above)(lambda: send_rows((2,), 1))
    for r in range(3, 13):
        features_of(r)

    half = _iota((1, 8, 512), 1) < 4

    def turned(x):
        return pltpu.roll(x.astype(F32), 4, 1)

    for load in loads[3:5]:
        load.wait()

    @pl.loop(1, 8)
    def _(tile):
        for src, dst in ((kv, ksh), (vv, vsh)):
            dst[tile] = jnp.where(half, turned(src[:, tile - 1]), turned(src[:, tile])).astype(BF)

    loads[5].wait()
    prob_feat = _prob_features(128)

    def two(x):
        return jnp.concatenate([_keep(low, x), _keep(jnp.logical_not(low), x)], axis=0)

    def front(s, t, p):
        lanes = pl.ds(128 * p, 128)
        k_rows = pl.ds(8 * t, 8)
        q_rows = pl.ds(4 * t, 12)
        keys = jnp.concatenate(
            [_flat(ksh[s, k_rows, :, lanes]), _flat(ksh[s + 1, k_rows, :, lanes])], axis=0
        )
        values = jnp.concatenate(
            [_flat(vsh[s, k_rows, :, lanes]), _flat(vsh[s + 1, k_rows, :, lanes])], axis=0
        )
        q2 = two(_flat(qv[q_rows, s, :, lanes]))
        g2 = two(_flat(gv[q_rows, s, :, lanes]))
        extra = _flat(aug[q_rows, s])
        a2 = jnp.concatenate(
            [_keep(head_keep[2 * p], extra), _keep(head_keep[2 * p + 1], extra)], axis=0
        )
        scores = _dot(
            jnp.concatenate([keys, feat[t]], axis=1),
            jnp.concatenate([q2, a2], axis=1),
            ((1,), (1,)),
        )
        prob_grad = _dot(
            jnp.concatenate([values, prob_feat], axis=1),
            jnp.concatenate([g2, a2], axis=1),
            ((1,), (1,)),
        )
        return scores, prob_grad, q2, g2, keys

    def middle(scores, prob_grad, q2, g2, keys):
        weights = jnp.exp2(scores * EXP_SCALE)
        score_grad = (weights * prob_grad).astype(BF)
        turned_grad = score_grad.T
        turned_grad = jnp.concatenate([turned_grad[:96], turned_grad[96:]], axis=1)
        return weights.astype(BF), score_grad, turned_grad, q2, g2, keys

    def back(s, t, p, weights, score_grad, turned_grad, q2, g2, keys):
        lanes = pl.ds(128 * p, 128)
        k_rows = pl.ds(8 * t, 8)
        d_keys = _dot(score_grad, q2, ((1,), (0,)))
        d_values = _dot(weights, g2, ((1,), (0,)))
        d_query = _dot(turned_grad, two(keys), ((1,), (0,)))
        for acc, d in ((dk_acc, d_keys), (dv_acc, d_values)):
            acc[s, k_rows, :, lanes] += d[:64].reshape(8, 8, 128)
            acc[s + 1, k_rows, :, lanes] += d[64:].reshape(8, 8, 128)
        return d_query

    def pipelined(todo, one, two_, three, use):
        n = len(todo)
        first, second = {}, {}
        for i in range(n + LAG1 + LAG2):
            if i < n:
                first[i] = one(*todo[i])
            j = i - LAG1
            if 0 <= j < n:
                second[j] = two_(*first.pop(j))
            j = i - LAG1 - LAG2
            if 0 <= j < n:
                use(j, three(*todo[j], *second.pop(j)))

    def strips(which):
        todo = [(s, t, p) for s in which for p in range(4) for t in range(2)]
        upper = [None]

        def use(j, d_query):
            s, t, p = todo[j]
            if t == 0:
                upper[0] = d_query
                return
            lanes = pl.ds(128 * p, 128)
            dq_acc[pl.ds(0, 4), s, :, lanes] = upper[0][:32].reshape(4, 8, 128)
            dq_acc[pl.ds(4, 8), s, :, lanes] = (upper[0][32:] + d_query[:64]).reshape(8, 8, 128)
            dq_acc[pl.ds(12, 4), s, :, lanes] = d_query[64:].reshape(4, 8, 128)

        pipelined(todo, front, middle, back, use)

    @pl.loop(0, 6 // PER)
    def _(i):
        strips([1 + PER * i + j for j in range(PER)])

    for what in range(2):
        for side in range(2):
            rim_copy(what, side).wait()
    for i, (src, dst) in enumerate(((kv, ksh), (vv, vsh))):
        dst[0] = jnp.where(half, turned(rim_in[0, i]), turned(src[:, 0])).astype(BF)
        dst[8] = jnp.where(half, turned(src[:, 7]), turned(rim_in[1, i])).astype(BF)

    strips([0, 7])

    prob_halo = _prob_features(96)

    def keys_of(ref, s, rows, lanes):
        return jnp.concatenate([_flat(ref[s + i, rows, :, lanes]) for i in range(3)], axis=0)

    def queries_of(ref, side, s, lanes):
        return jnp.concatenate([_flat(ref[side, :, s + i, :, lanes]) for i in range(2)], axis=0)

    def halo_front(s, side, p):
        lanes = pl.ds(128 * p, 128)
        rows = pl.ds(12 * side, 4)
        keys = keys_of(ksh, s, rows, lanes)
        values = keys_of(vsh, s, rows, lanes)
        q2 = two(queries_of(q_halo, side, s, lanes))
        g2 = two(queries_of(g_halo, side, s, lanes))
        extra = queries_of(a_halo, side, s, pl.ds(0, 128))
        a2 = jnp.concatenate(
            [_keep(head_keep[2 * p], extra), _keep(head_keep[2 * p + 1], extra)], axis=0
        )
        scores = _dot(
            jnp.concatenate([keys, feat_halo[side]], axis=1),
            jnp.concatenate([q2, a2], axis=1),
            ((1,), (1,)),
        )
        prob_grad = _dot(
            jnp.concatenate([values, prob_halo], axis=1),
            jnp.concatenate([g2, a2], axis=1),
            ((1,), (1,)),
        )
        return scores, prob_grad, q2, g2, keys

    def halo_middle(scores, prob_grad, q2, g2, keys):
        weights = jnp.exp2(scores * EXP_SCALE)
        score_grad = (weights * prob_grad).astype(BF)
        return weights.astype(BF), score_grad, score_grad.T, q2, g2, keys

    def halo_back(s, side, p, weights, score_grad, turned_grad, q2, g2, keys):
        lanes = pl.ds(128 * p, 128)
        rows = pl.ds(12 * side, 4)
        d_keys = _dot(score_grad, q2, ((1,), (0,)))
        d_values = _dot(weights, g2, ((1,), (0,)))
        d_query = _dot(turned_grad, keys, ((1,), (0,)))
        d_query = jnp.where(low, d_query[:64], d_query[64:]) * 0.125
        for i in range(2):
            part = d_query[32 * i : 32 * i + 24].reshape(3, 8, 128)
            dq_send[side, :, s + i, :, lanes] = part.astype(BF)
        for acc, d in ((dk_acc, d_keys), (dv_acc, d_values)):
            for i in range(3):
                acc[s + i, rows, :, lanes] += d[32 * i : 32 * i + 32].reshape(4, 8, 128)

    def halo(chunk, side):
        for what in range(3):
            row_copy(what, chunk, side).wait_recv()
        todo = [(s, side, p) for s in range(chunk * width, (chunk + 1) * width, 2) for p in range(4)]
        pipelined(todo, halo_front, halo_middle, halo_back, lambda j, done: None)
        back_copy(chunk, side).start()

    for chunk in range(CHUNKS):
        pl.when(has_above)(functools.partial(halo, chunk, 0))
        pl.when(has_below)(functools.partial(halo, chunk, 1))

    half8 = _iota((1, 8, 512), 1) < 4
    for what, acc in enumerate((dk_acc, dv_acc)):
        scale = 0.125 if what == 0 else 1.0
        for i in range(8):
            a, b = acc[8, 2 * i], acc[8, 2 * i + 1]
            rim_send[0, what, i] = (
                jnp.where(half8[0], pltpu.roll(a, 4, 0), b) * scale
            ).astype(BF)
            a, b = acc[0, 2 * i], acc[0, 2 * i + 1]
            rim_send[1, what, i] = (
                jnp.where(half8[0], a, pltpu.roll(b, 4, 0)) * scale
            ).astype(BF)
        for side in range(2):
            grad_copy(what, side).start()

    @pl.loop(3, 13)
    def _(r):
        dq_out[r] = (dq_acc[r] * 0.125).astype(BF)

    def merged(acc, j, scale):
        return pltpu.roll(jnp.where(half, acc[j + 1], acc[j]), 4, 1) * scale

    @pl.loop(1, 7)
    def _(j):
        dk_out[:, j] = merged(dk_acc, j, 0.125).astype(BF)
        dv_out[:, j] = merged(dv_acc, j, 1.0).astype(BF)

    for what in range(2):
        for side in range(2):
            grad_copy(what, side).wait()
    for what, (acc, out) in enumerate(((dk_acc, dk_out), (dv_acc, dv_out))):
        scale = 0.125 if what == 0 else 1.0
        edge = merged(acc, 0, scale)
        came = rim_recv[0, what].astype(F32)
        spun = pltpu.roll(came, 4, 1)
        for i in range(8):
            out[2 * i, 0] = (edge[2 * i] + _keep(half8[0], came[i])).astype(BF)
            out[2 * i + 1, 0] = (edge[2 * i + 1] + _keep(half8[0], spun[i])).astype(BF)
        edge = merged(acc, 7, scale)
        came = rim_recv[1, what].astype(F32)
        spun = pltpu.roll(came, 4, 1)
        for i in range(8):
            out[2 * i, 7] = (edge[2 * i] + _keep(jnp.logical_not(half8[0]), spun[i])).astype(BF)
            out[2 * i + 1, 7] = (
                edge[2 * i + 1] + _keep(jnp.logical_not(half8[0]), came[i])
            ).astype(BF)

    def finish(side, rows):
        @pl.when(has_above if side == 0 else has_below)
        def _():
            for chunk in range(CHUNKS):
                back_copy(chunk, 1 - side).wait_recv()
            for r in range(3):
                dq_out[rows + r] = (
                    dq_acc[rows + r] * 0.125 + dq_recv[side, r].astype(F32)
                ).astype(BF)

        @pl.when(jnp.logical_not(has_above if side == 0 else has_below))
        def _():
            for r in range(3):
                dq_out[rows + r] = (dq_acc[rows + r] * 0.125).astype(BF)

    finish(0, 0)
    finish(1, 13)

    def drain(send_side, back_side):
        for chunk in range(CHUNKS):
            for what in range(3):
                row_copy(what, chunk, send_side).wait_send()
            back_copy(chunk, back_side).wait_send()

    pl.when(has_below)(lambda: drain(0, 1))
    pl.when(has_above)(lambda: drain(1, 0))


def solution(mesh):
    n_lat, n_lon = mesh.shape["lat"], mesh.shape["lon"]

    def per_device(query_tok, key_tok, value_tok, output_tok, grad_output, log_totals):
        def tiled(x):
            return x.reshape(16, 8, 8, 512)

        dma = pltpu.SemaphoreType.DMA
        token = (16, 8, 8, 512)
        shifted = (9, 16, 8, 512)
        outs = pl.pallas_call(
            functools.partial(kernel, n_lat, n_lon),
            out_shape=[jax.ShapeDtypeStruct(token, BF)] * 3,
            in_specs=[pl.BlockSpec(memory_space=pl.ANY)] * 6,
            out_specs=[pl.BlockSpec(memory_space=pltpu.VMEM)] * 3,
            scratch_shapes=[
                pltpu.VMEM(token, BF),
                pltpu.VMEM(token, BF),
                pltpu.VMEM(token, BF),
                pltpu.VMEM(token, BF),
                pltpu.VMEM(token, BF),
                pltpu.VMEM((128, 64), F32),
                pltpu.VMEM((16, 8, 8, 128), BF),
                pltpu.VMEM(shifted, BF),
                pltpu.VMEM(shifted, BF),
                pltpu.VMEM(token, F32),
                pltpu.VMEM(shifted, F32),
                pltpu.VMEM(shifted, F32),
                pltpu.VMEM((2, 128, 128), BF),
                pltpu.VMEM((2, 96, 128), BF),
                pltpu.VMEM((2, 2, 16, 8, 512), BF),
                pltpu.VMEM((2, 4, 8, 8, 512), BF),
                pltpu.VMEM((2, 4, 8, 8, 512), BF),
                pltpu.VMEM((2, 4, 8, 8, 128), BF),
                pltpu.VMEM((2, 3, 8, 8, 512), BF),
                pltpu.VMEM((2, 3, 8, 8, 512), BF),
                pltpu.VMEM((2, 2, 8, 8, 512), BF),
                pltpu.VMEM((2, 2, 8, 8, 512), BF),
                dma((6,)),
                dma((2, 2, 2)),
                dma((2, 3, CHUNKS, 2)),
                dma((2, CHUNKS, 2)),
                dma((2, 2, 2)),
            ],
            compiler_params=pltpu.CompilerParams(
                collective_id=0,
                has_side_effects=True,
                vmem_limit_bytes=56 * 1024 * 1024,
            ),
        )(
            tiled(query_tok),
            tiled(key_tok),
            tiled(value_tok),
            tiled(output_tok),
            tiled(grad_output),
            log_totals.reshape(128, 64),
        )
        return tuple(x.reshape(16, 64, 512) for x in outs)

    return jax.shard_map(
        per_device,
        mesh=mesh,
        in_specs=(P("lat", "lon", None),) * 5 + (P(None, "lat", "lon"),),
        out_specs=(P("lat", "lon", None),) * 3,
        check_vma=False,
    )
```

```python
import functools

import jax
import jax.numpy as jnp
from jax import lax
from jax.experimental import pallas as pl
from jax.experimental.pallas import tpu as pltpu
from jax.sharding import PartitionSpec as P

MESH = pl.DeviceIdType.MESH
BF = jnp.bfloat16
F32 = jnp.float32
BIG = 32768.0
EXP_SCALE = 0.125 * 1.4426950408889634
CHUNKS = 2
LAG1 = 2
LAG2 = 2
PER = 2
RELAY_STEPS = (((0, 0), (1, 0)), ((0, 1), (2, 0)), ((1, 1), (2, 1)))


def _iota(shape, dim):
    return lax.broadcasted_iota(jnp.int32, shape, dim)


def _dot(a, b, dims):
    return lax.dot_general(a, b, (dims, ((), ())), preferred_element_type=F32)


def _keep(mask, x):
    return jnp.where(mask, x, jnp.zeros_like(x))


def _flat(x):
    return x.reshape(-1, x.shape[-1])


def _key_features(base, row0, rows, q_base, total, tiles, spread):
    shape = (tiles * rows * 8, 128)
    key = _iota(shape, 0)
    lane = _iota(shape, 1)
    tile = key // (rows * 8)
    k_row = base + row0 + key // 8 % rows
    k_col = tile * 8 + key % 8
    group, slot = lane // 16, lane % 16
    q_row = q_base + 2 * group + slot - 6
    first = jnp.clip(q_row - 3, 0, total - 7)
    row_ok = (k_row >= first) & (k_row < first + 7)
    gap = k_col - 4 - group - jnp.where(slot == 9, spread, 0)
    col_ok = (gap >= -3) & (gap <= 3)
    row_slot = (slot == 6) | (slot == 7)
    bad = (row_slot & jnp.logical_not(row_ok)) | (
        ((slot == 8) | (slot == 9)) & jnp.logical_not(col_ok)
    )
    value = jnp.where(bad, -BIG, jnp.where(slot < 3, -8.0, 0.0))
    return value.astype(BF)


def _prob_features(keys):
    slot = _iota((keys, 128), 1) % 16
    return jnp.where((slot >= 3) & (slot < 6), -1.0, 0.0).astype(BF)


def _split3(x):
    a = x.astype(BF).astype(F32)
    rest = x - a
    b = rest.astype(BF).astype(F32)
    return a, b, rest - b


def kernel(
    n_lat,
    n_lon,
    q_hbm,
    k_hbm,
    v_hbm,
    o_hbm,
    g_hbm,
    lt_hbm,
    dq_out,
    dk_out,
    dv_out,
    qv,
    kv,
    vv,
    ov,
    gv,
    ltv,
    aug,
    ksh,
    vsh,
    dq_acc,
    dk_acc,
    dv_acc,
    feat,
    feat_halo,
    rim_in,
    q_halo,
    g_halo,
    a_halo,
    dq_send,
    dq_recv,
    rim_send,
    rim_recv,
    load_sem,
    rim_sems,
    row_sems,
    back_sems,
    grad_sems,
):
    lat = lax.axis_index("lat")
    lon = lax.axis_index("lon")
    left = (lat, lax.rem(lon + n_lon - 1, n_lon))
    right = (lat, lax.rem(lon + 1, n_lon))
    above = (lat - 1, lon)
    below = (lat + 1, lon)
    has_above = lat > 0
    has_below = lat < n_lat - 1
    middle_band = n_lat // 2
    relayed = n_lat >= 4 and n_lat % 2 == 0 and n_lon % 4 == 0
    across = lon + 2 - 4 * (lon // 2 % 2) if relayed else lon
    near_middle = [lat == middle_band - 1, lat == middle_band] if relayed else [False, False]
    is_relay = [lat == 0, lat == n_lat - 1] if relayed else [False, False]

    def as_int(condition):
        return jnp.where(condition, 1, 0)

    total = n_lat * 16
    base = lat * 16
    width = 8 // CHUNKS

    loads = [
        pltpu.make_async_copy(src, dst, load_sem.at[i])
        for i, (src, dst) in enumerate(
            ((g_hbm, gv), (o_hbm, ov), (lt_hbm, ltv), (k_hbm, kv), (v_hbm, vv), (q_hbm, qv))
        )
    ]
    for load in loads:
        load.start()

    barrier = pltpu.get_barrier_semaphore()

    def greet(device):
        pl.semaphore_signal(barrier, inc=1, device_id=device, device_id_type=MESH)

    greet(left)
    greet(right)
    pl.when(has_above)(lambda: greet(above))
    pl.when(has_below)(lambda: greet(below))
    peers = 2 + as_int(has_above) + as_int(has_below)
    if relayed:
        for place, partners in (
            (near_middle[0] | near_middle[1], (0, n_lat - 1)),
            (is_relay[0] | is_relay[1], (middle_band - 1, middle_band)),
        ):
            peers += 2 * as_int(place)
            for partner in partners:
                pl.when(place)(functools.partial(greet, (partner, across)))
    pl.semaphore_wait(barrier, peers)

    def remote(src, dst, sems, index, device, landing=None):
        return pltpu.make_async_remote_copy(
            src_ref=src,
            dst_ref=dst,
            send_sem=sems.at[(0,) + index],
            recv_sem=sems.at[(1,) + (index if landing is None else landing)],
            device_id=device,
            device_id_type=MESH,
        )

    row_buffers = ((q_hbm, q_halo), (g_hbm, g_halo), (aug, a_halo))

    def row_copy(what, chunk, side):
        src, dst = row_buffers[what]
        rows = pl.ds(13, 3) if side == 0 else pl.ds(0, 3)
        strips = pl.ds(chunk * width, width)
        device, slot = (below, above)[side], side
        if relayed:
            turn = as_int(near_middle[side])
            hop = middle_band - 1 if side == 1 else n_lat - 1 - middle_band
            direction = 1 - 2 * side
            device = (
                lat + direction * (1 + turn * hop),
                lon + turn * (across - lon),
            )
            slot = side + direction * turn
        return remote(
            src.at[rows, strips],
            dst.at[slot, pl.ds(0, 3), strips],
            row_sems,
            (what, chunk, side),
            device,
            (what, chunk, slot),
        )

    def row_forward(what, chunk, side):
        buffer = row_buffers[what][1]
        strips = pl.ds(chunk * width, width)
        return remote(
            buffer.at[side, pl.ds(0, 3), strips],
            buffer.at[1 - side, pl.ds(0, 3), strips],
            row_sems,
            (what, chunk, 1 - side),
            (middle_band - 1 + side, across),
        )

    def await_rows(what, chunk, side):
        buffer = row_buffers[what][1]
        rows = buffer.at[side, pl.ds(0, 3), pl.ds(chunk * width, width)]
        remote(rows, rows, row_sems, (what, chunk, side), left).wait_recv()

    def forward(pieces):
        if not relayed:
            return
        for side in range(2):

            @pl.when(is_relay[side])
            def _():
                for what, chunk in pieces:
                    await_rows(what, chunk, side)
                    row_forward(what, chunk, side).start()

    def rim_copy(what, side):
        src = (k_hbm, v_hbm)[what]
        return remote(
            src.at[:, 7 if side == 0 else 0, pl.ds(4 if side == 0 else 0, 4)],
            rim_in.at[side, what, :, pl.ds(4 if side == 0 else 0, 4)],
            rim_sems,
            (what, side),
            right if side == 0 else left,
        )

    def back_copy(chunk, side):
        strips = pl.ds(chunk * width, width)
        return remote(
            dq_send.at[side, :, strips],
            dq_recv.at[1 - side, :, strips],
            back_sems,
            (chunk, 1 - side),
            above if side == 0 else below,
        )

    def grad_copy(what, side):
        return remote(
            rim_send.at[side, what],
            rim_recv.at[side, what],
            grad_sems,
            (what, side),
            right if side == 0 else left,
        )

    def send_rows(whats, side):
        for chunk in range(CHUNKS):
            for what in whats:
                row_copy(what, chunk, side).start()

    pl.when(has_below)(lambda: send_rows((0, 1), 0))
    pl.when(has_above)(lambda: send_rows((0, 1), 1))
    for what in range(2):
        for side in range(2):
            rim_copy(what, side).start()

    slot16 = _iota((1, 128), 1) % 16
    group16 = _iota((1, 128), 1) // 16
    low = _iota((1, 128), 1) < 64
    head_keep = [(group16 == h) | (slot16 >= 6) for h in range(8)]
    for t in range(2):
        feat[t] = _key_features(base, 8 * t, 8, base, total, 2, 0)
    feat_halo[0] = _key_features(base, 0, 4, base - 16, total, 3, 8)
    feat_halo[1] = _key_features(base, 12, 4, base + 16, total, 3, 8)

    @pl.loop(0, 9)
    def _(tile):
        dk_acc[tile] = jnp.zeros((16, 8, 512), F32)
        dv_acc[tile] = jnp.zeros((16, 8, 512), F32)

    for side in range(2):
        q_halo[side, 3] = jnp.zeros((8, 8, 512), BF)
        g_halo[side, 3] = jnp.zeros((8, 8, 512), BF)
        a_halo[side, 3] = jnp.zeros((8, 8, 128), BF)

    feature = _iota((512, 128), 0)
    lane = _iota((512, 128), 1)
    spread = jnp.where(
        (lane // 16 == feature // 64) & (lane % 16 >= 3) & (lane % 16 < 6), 1.0, 0.0
    ).astype(BF)
    for load in loads[:3]:
        load.wait()
    parts = _split3(ltv[...].T)
    column = _iota((64, 128), 0) % 8
    group = _iota((64, 128), 1) // 16
    slot = _iota((64, 128), 1) % 16
    odd = _iota((64, 128), 0) // 8 % 2
    col_hot = jnp.where((slot == 8 + odd) & (group == column), 1.0, 0.0)

    def features_of(r):
        product = _flat(gv[r].astype(F32)) * _flat(ov[r].astype(F32))
        high = product.astype(BF)
        rest = (product - high.astype(F32)).astype(BF)
        delta = _dot(high, spread, ((1,), (0,))) + _dot(rest, spread, ((1,), (0,)))
        d0, d1, d2 = _split3(delta)
        rolled = [pltpu.roll(part, (i - r) % 128, 1) for i, part in enumerate(parts)]
        value = jnp.where((slot >= 6) & (slot < 8) & (2 * group + slot - 6 == r), 1.0, col_hot)
        for i, x in enumerate(rolled + [d0, d1, d2]):
            value = jnp.where(slot == i, x, value)
        aug[r] = value.astype(BF).reshape(8, 8, 128)

    for r in (13, 14, 15):
        features_of(r)
    pl.when(has_below)(lambda: send_rows((2,), 0))
    for r in (0, 1, 2):
        features_of(r)
    pl.when(has_above)(lambda: send_rows((2,), 1))
    for r in range(3, 13):
        features_of(r)

    half = _iota((1, 8, 512), 1) < 4

    def turned(x):
        return pltpu.roll(x.astype(F32), 4, 1)

    for load in loads[3:5]:
        load.wait()

    @pl.loop(1, 8)
    def _(tile):
        for src, dst in ((kv, ksh), (vv, vsh)):
            dst[tile] = jnp.where(half, turned(src[:, tile - 1]), turned(src[:, tile])).astype(BF)

    loads[5].wait()
    prob_feat = _prob_features(128)

    def two(x):
        return jnp.concatenate([_keep(low, x), _keep(jnp.logical_not(low), x)], axis=0)

    def front(s, t, p):
        lanes = pl.ds(128 * p, 128)
        k_rows = pl.ds(8 * t, 8)
        q_rows = pl.ds(4 * t, 12)
        keys = jnp.concatenate(
            [_flat(ksh[s, k_rows, :, lanes]), _flat(ksh[s + 1, k_rows, :, lanes])], axis=0
        )
        values = jnp.concatenate(
            [_flat(vsh[s, k_rows, :, lanes]), _flat(vsh[s + 1, k_rows, :, lanes])], axis=0
        )
        q2 = two(_flat(qv[q_rows, s, :, lanes]))
        g2 = two(_flat(gv[q_rows, s, :, lanes]))
        extra = _flat(aug[q_rows, s])
        a2 = jnp.concatenate(
            [_keep(head_keep[2 * p], extra), _keep(head_keep[2 * p + 1], extra)], axis=0
        )
        scores = _dot(
            jnp.concatenate([keys, feat[t]], axis=1),
            jnp.concatenate([q2, a2], axis=1),
            ((1,), (1,)),
        )
        prob_grad = _dot(
            jnp.concatenate([values, prob_feat], axis=1),
            jnp.concatenate([g2, a2], axis=1),
            ((1,), (1,)),
        )
        return scores, prob_grad, q2, g2, keys

    def middle(scores, prob_grad, q2, g2, keys):
        weights = jnp.exp2(scores * EXP_SCALE)
        score_grad = (weights * prob_grad).astype(BF)
        turned_grad = score_grad.T
        turned_grad = jnp.concatenate([turned_grad[:96], turned_grad[96:]], axis=1)
        return weights.astype(BF), score_grad, turned_grad, q2, g2, keys

    def back(s, t, p, weights, score_grad, turned_grad, q2, g2, keys):
        lanes = pl.ds(128 * p, 128)
        k_rows = pl.ds(8 * t, 8)
        d_keys = _dot(score_grad, q2, ((1,), (0,)))
        d_values = _dot(weights, g2, ((1,), (0,)))
        d_query = _dot(turned_grad, two(keys), ((1,), (0,)))
        for acc, d in ((dk_acc, d_keys), (dv_acc, d_values)):
            acc[s, k_rows, :, lanes] += d[:64].reshape(8, 8, 128)
            acc[s + 1, k_rows, :, lanes] += d[64:].reshape(8, 8, 128)
        return d_query

    def pipelined(todo, one, two_, three, use):
        n = len(todo)
        first, second = {}, {}
        for i in range(n + LAG1 + LAG2):
            if i < n:
                first[i] = one(*todo[i])
            j = i - LAG1
            if 0 <= j < n:
                second[j] = two_(*first.pop(j))
            j = i - LAG1 - LAG2
            if 0 <= j < n:
                use(j, three(*todo[j], *second.pop(j)))

    def strips(which):
        todo = [(s, t, p) for s in which for p in range(4) for t in range(2)]
        upper = [None]

        def use(j, d_query):
            s, t, p = todo[j]
            if t == 0:
                upper[0] = d_query
                return
            lanes = pl.ds(128 * p, 128)
            dq_acc[pl.ds(0, 4), s, :, lanes] = upper[0][:32].reshape(4, 8, 128)
            dq_acc[pl.ds(4, 8), s, :, lanes] = (upper[0][32:] + d_query[:64]).reshape(8, 8, 128)
            dq_acc[pl.ds(12, 4), s, :, lanes] = d_query[64:].reshape(4, 8, 128)

        pipelined(todo, front, middle, back, use)

    @pl.loop(0, 6 // PER)
    def _(i):
        strips([1 + PER * i + j for j in range(PER)])
        for step, pieces in enumerate(RELAY_STEPS):
            pl.when(i == step)(functools.partial(forward, pieces))

    for what in range(2):
        for side in range(2):
            rim_copy(what, side).wait()
    for i, (src, dst) in enumerate(((kv, ksh), (vv, vsh))):
        dst[0] = jnp.where(half, turned(rim_in[0, i]), turned(src[:, 0])).astype(BF)
        dst[8] = jnp.where(half, turned(src[:, 7]), turned(rim_in[1, i])).astype(BF)

    strips([0, 7])

    prob_halo = _prob_features(96)

    def keys_of(ref, s, rows, lanes):
        return jnp.concatenate([_flat(ref[s + i, rows, :, lanes]) for i in range(3)], axis=0)

    def queries_of(ref, side, s, lanes):
        return jnp.concatenate([_flat(ref[side, :, s + i, :, lanes]) for i in range(2)], axis=0)

    def halo_front(s, side, p):
        lanes = pl.ds(128 * p, 128)
        rows = pl.ds(12 * side, 4)
        keys = keys_of(ksh, s, rows, lanes)
        values = keys_of(vsh, s, rows, lanes)
        q2 = two(queries_of(q_halo, side, s, lanes))
        g2 = two(queries_of(g_halo, side, s, lanes))
        extra = queries_of(a_halo, side, s, pl.ds(0, 128))
        a2 = jnp.concatenate(
            [_keep(head_keep[2 * p], extra), _keep(head_keep[2 * p + 1], extra)], axis=0
        )
        scores = _dot(
            jnp.concatenate([keys, feat_halo[side]], axis=1),
            jnp.concatenate([q2, a2], axis=1),
            ((1,), (1,)),
        )
        prob_grad = _dot(
            jnp.concatenate([values, prob_halo], axis=1),
            jnp.concatenate([g2, a2], axis=1),
            ((1,), (1,)),
        )
        return scores, prob_grad, q2, g2, keys

    def halo_middle(scores, prob_grad, q2, g2, keys):
        weights = jnp.exp2(scores * EXP_SCALE)
        score_grad = (weights * prob_grad).astype(BF)
        return weights.astype(BF), score_grad, score_grad.T, q2, g2, keys

    def halo_back(s, side, p, weights, score_grad, turned_grad, q2, g2, keys):
        lanes = pl.ds(128 * p, 128)
        rows = pl.ds(12 * side, 4)
        d_keys = _dot(score_grad, q2, ((1,), (0,)))
        d_values = _dot(weights, g2, ((1,), (0,)))
        d_query = _dot(turned_grad, keys, ((1,), (0,)))
        d_query = jnp.where(low, d_query[:64], d_query[64:]) * 0.125
        for i in range(2):
            part = d_query[32 * i : 32 * i + 24].reshape(3, 8, 128)
            dq_send[side, :, s + i, :, lanes] = part.astype(BF)
        for acc, d in ((dk_acc, d_keys), (dv_acc, d_values)):
            for i in range(3):
                acc[s + i, rows, :, lanes] += d[32 * i : 32 * i + 32].reshape(4, 8, 128)

    def halo(chunk, side):
        for what in range(3):
            await_rows(what, chunk, side)
        todo = [(s, side, p) for s in range(chunk * width, (chunk + 1) * width, 2) for p in range(4)]
        pipelined(todo, halo_front, halo_middle, halo_back, lambda j, done: None)
        back_copy(chunk, side).start()

    for chunk in range(CHUNKS):
        pl.when(has_above)(functools.partial(halo, chunk, 0))
        pl.when(has_below)(functools.partial(halo, chunk, 1))

    half8 = _iota((1, 8, 512), 1) < 4
    for what, acc in enumerate((dk_acc, dv_acc)):
        scale = 0.125 if what == 0 else 1.0
        for i in range(8):
            a, b = acc[8, 2 * i], acc[8, 2 * i + 1]
            rim_send[0, what, i] = (
                jnp.where(half8[0], pltpu.roll(a, 4, 0), b) * scale
            ).astype(BF)
            a, b = acc[0, 2 * i], acc[0, 2 * i + 1]
            rim_send[1, what, i] = (
                jnp.where(half8[0], a, pltpu.roll(b, 4, 0)) * scale
            ).astype(BF)
        for side in range(2):
            grad_copy(what, side).start()

    @pl.loop(3, 13)
    def _(r):
        dq_out[r] = (dq_acc[r] * 0.125).astype(BF)

    def merged(acc, j, scale):
        return pltpu.roll(jnp.where(half, acc[j + 1], acc[j]), 4, 1) * scale

    @pl.loop(1, 7)
    def _(j):
        dk_out[:, j] = merged(dk_acc, j, 0.125).astype(BF)
        dv_out[:, j] = merged(dv_acc, j, 1.0).astype(BF)

    for what in range(2):
        for side in range(2):
            grad_copy(what, side).wait()
    for what, (acc, out) in enumerate(((dk_acc, dk_out), (dv_acc, dv_out))):
        scale = 0.125 if what == 0 else 1.0
        edge = merged(acc, 0, scale)
        came = rim_recv[0, what].astype(F32)
        spun = pltpu.roll(came, 4, 1)
        for i in range(8):
            out[2 * i, 0] = (edge[2 * i] + _keep(half8[0], came[i])).astype(BF)
            out[2 * i + 1, 0] = (edge[2 * i + 1] + _keep(half8[0], spun[i])).astype(BF)
        edge = merged(acc, 7, scale)
        came = rim_recv[1, what].astype(F32)
        spun = pltpu.roll(came, 4, 1)
        for i in range(8):
            out[2 * i, 7] = (edge[2 * i] + _keep(jnp.logical_not(half8[0]), spun[i])).astype(BF)
            out[2 * i + 1, 7] = (
                edge[2 * i + 1] + _keep(jnp.logical_not(half8[0]), came[i])
            ).astype(BF)

    def finish(side, rows):
        @pl.when(has_above if side == 0 else has_below)
        def _():
            for chunk in range(CHUNKS):
                back_copy(chunk, 1 - side).wait_recv()
            for r in range(3):
                dq_out[rows + r] = (
                    dq_acc[rows + r] * 0.125 + dq_recv[side, r].astype(F32)
                ).astype(BF)

        @pl.when(jnp.logical_not(has_above if side == 0 else has_below))
        def _():
            for r in range(3):
                dq_out[rows + r] = (dq_acc[rows + r] * 0.125).astype(BF)

    finish(0, 0)
    finish(1, 13)

    def drain(send_side, back_side):
        for chunk in range(CHUNKS):
            for what in range(3):
                row_copy(what, chunk, send_side).wait_send()
            back_copy(chunk, back_side).wait_send()

    if relayed:
        for side in range(2):

            @pl.when(is_relay[side])
            def _():
                for pieces in RELAY_STEPS:
                    for what, chunk in pieces:
                        row_forward(what, chunk, side).wait_send()

    pl.when(has_below)(lambda: drain(0, 1))
    pl.when(has_above)(lambda: drain(1, 0))


def store_kernel(a, b, c, a_out, b_out, c_out, sem):
    copies = [
        pltpu.make_async_copy(src, dst, sem.at[i])
        for i, (src, dst) in enumerate(((a, a_out), (b, b_out), (c, c_out)))
    ]
    for copy in copies:
        copy.start()
    for copy in copies:
        copy.wait()


def solution(mesh):
    n_lat, n_lon = mesh.shape["lat"], mesh.shape["lon"]

    def per_device(query_tok, key_tok, value_tok, output_tok, grad_output, log_totals):
        def tiled(x):
            return x.reshape(16, 8, 8, 512)

        dma = pltpu.SemaphoreType.DMA
        token = (16, 8, 8, 512)
        shifted = (9, 16, 8, 512)
        outs = pl.pallas_call(
            functools.partial(kernel, n_lat, n_lon),
            out_shape=[pltpu.VMEM(token, BF)] * 3,
            in_specs=[pl.BlockSpec(memory_space=pltpu.HBM)] * 6,
            out_specs=[pl.BlockSpec(memory_space=pltpu.VMEM)] * 3,
            scratch_shapes=[
                pltpu.VMEM(token, BF),
                pltpu.VMEM(token, BF),
                pltpu.VMEM(token, BF),
                pltpu.VMEM(token, BF),
                pltpu.VMEM(token, BF),
                pltpu.VMEM((128, 64), F32),
                pltpu.VMEM((16, 8, 8, 128), BF),
                pltpu.VMEM(shifted, BF),
                pltpu.VMEM(shifted, BF),
                pltpu.VMEM(token, F32),
                pltpu.VMEM(shifted, F32),
                pltpu.VMEM(shifted, F32),
                pltpu.VMEM((2, 128, 128), BF),
                pltpu.VMEM((2, 96, 128), BF),
                pltpu.VMEM((2, 2, 16, 8, 512), BF),
                pltpu.VMEM((2, 4, 8, 8, 512), BF),
                pltpu.VMEM((2, 4, 8, 8, 512), BF),
                pltpu.VMEM((2, 4, 8, 8, 128), BF),
                pltpu.VMEM((2, 3, 8, 8, 512), BF),
                pltpu.VMEM((2, 3, 8, 8, 512), BF),
                pltpu.VMEM((2, 2, 8, 8, 512), BF),
                pltpu.VMEM((2, 2, 8, 8, 512), BF),
                dma((6,)),
                dma((2, 2, 2)),
                dma((2, 3, CHUNKS, 2)),
                dma((2, CHUNKS, 2)),
                dma((2, 2, 2)),
            ],
            compiler_params=pltpu.CompilerParams(
                collective_id=0,
                has_side_effects=True,
                vmem_limit_bytes=56 * 1024 * 1024,
            ),
        )(
            tiled(query_tok),
            tiled(key_tok),
            tiled(value_tok),
            tiled(output_tok),
            tiled(grad_output),
            log_totals.reshape(128, 64),
        )
        outs = pl.pallas_call(
            store_kernel,
            out_shape=[jax.ShapeDtypeStruct(token, BF)] * 3,
            in_specs=[pl.BlockSpec(memory_space=pltpu.VMEM)] * 3,
            out_specs=[pl.BlockSpec(memory_space=pltpu.HBM)] * 3,
            scratch_shapes=[dma((3,))],
            compiler_params=pltpu.CompilerParams(vmem_limit_bytes=8 * 1024 * 1024),
        )(*outs)
        return tuple(x.reshape(16, 64, 512) for x in outs)

    return jax.shard_map(
        per_device,
        mesh=mesh,
        in_specs=(P("lat", "lon", None),) * 5 + (P(None, "lat", "lon"),),
        out_specs=(P("lat", "lon", None),) * 3,
        check_vma=False,
    )
```

```python
import functools

import jax
import jax.numpy as jnp
from jax import lax
from jax.experimental import pallas as pl
from jax.experimental.pallas import tpu as pltpu
from jax.sharding import PartitionSpec as P

MESH = pl.DeviceIdType.MESH
BF = jnp.bfloat16
F32 = jnp.float32
BIG = 32768.0
EXP_SCALE = 0.125 * 1.4426950408889634
CHUNKS = 2
LAG1 = 2
LAG2 = 2
RELAY_STEPS = (((0, 0), (1, 0)), ((0, 1), (2, 0)), ((1, 1), (2, 1)))


def _iota(shape, dim):
    return lax.broadcasted_iota(jnp.int32, shape, dim)


def _dot(a, b, dims):
    return lax.dot_general(a, b, (dims, ((), ())), preferred_element_type=F32)


def _keep(mask, x):
    return jnp.where(mask, x, jnp.zeros_like(x))


def _flat(x):
    return x.reshape(-1, x.shape[-1])


def _key_features(base, row0, rows, q_base, total, tiles, spread):
    shape = (tiles * rows * 8, 128)
    key = _iota(shape, 0)
    lane = _iota(shape, 1)
    tile = key // (rows * 8)
    k_row = base + row0 + key // 8 % rows
    k_col = tile * 8 + key % 8
    group, slot = lane // 16, lane % 16
    q_row = q_base + 2 * group + slot - 6
    first = jnp.clip(q_row - 3, 0, total - 7)
    row_ok = (k_row >= first) & (k_row < first + 7)
    gap = k_col - 4 - group - jnp.where(slot == 9, spread, 0)
    col_ok = (gap >= -3) & (gap <= 3)
    row_slot = (slot == 6) | (slot == 7)
    bad = (row_slot & jnp.logical_not(row_ok)) | (
        ((slot == 8) | (slot == 9)) & jnp.logical_not(col_ok)
    )
    value = jnp.where(bad, -BIG, jnp.where(slot < 3, -8.0, 0.0))
    return value.astype(BF)


def _prob_features(keys):
    slot = _iota((keys, 128), 1) % 16
    return jnp.where((slot >= 3) & (slot < 6), -1.0, 0.0).astype(BF)


def _split3(x):
    a = x.astype(BF).astype(F32)
    rest = x - a
    b = rest.astype(BF).astype(F32)
    return a, b, rest - b


def kernel(
    n_lat,
    n_lon,
    q_hbm,
    k_hbm,
    v_hbm,
    o_hbm,
    g_hbm,
    lt_hbm,
    dq_out,
    dk_out,
    dv_out,
    qv,
    kv,
    vv,
    ov,
    gv,
    ltv,
    aug,
    ksh,
    vsh,
    dq_acc,
    dk_acc,
    dv_acc,
    feat,
    feat_halo,
    rim_in,
    q_halo,
    g_halo,
    a_halo,
    dq_send,
    dq_recv,
    rim_send,
    rim_recv,
    load_sem,
    rim_sems,
    row_sems,
    back_sems,
    grad_sems,
    ready,
):
    lat = lax.axis_index("lat")
    lon = lax.axis_index("lon")
    left = (lat, lax.rem(lon + n_lon - 1, n_lon))
    right = (lat, lax.rem(lon + 1, n_lon))
    above = (lat - 1, lon)
    below = (lat + 1, lon)
    has_above = lat > 0
    has_below = lat < n_lat - 1
    middle_band = n_lat // 2
    relayed = n_lat >= 4 and n_lat % 2 == 0 and n_lon % 4 == 0
    across = lon + 2 - 4 * (lon // 2 % 2) if relayed else lon
    near_middle = [lat == middle_band - 1, lat == middle_band] if relayed else [False, False]
    is_relay = [lat == 0, lat == n_lat - 1] if relayed else [False, False]

    def as_int(condition):
        return jnp.where(condition, 1, 0)

    total = n_lat * 16
    base = lat * 16
    width = 8 // CHUNKS

    loads = [
        pltpu.make_async_copy(src, dst, load_sem.at[i])
        for i, (src, dst) in enumerate(
            ((g_hbm, gv), (o_hbm, ov), (lt_hbm, ltv), (k_hbm, kv), (v_hbm, vv), (q_hbm, qv))
        )
    ]
    for load in loads:
        load.start()

    barrier = pltpu.get_barrier_semaphore()

    def greet(device):
        pl.semaphore_signal(barrier, inc=1, device_id=device, device_id_type=MESH)

    greet(left)
    greet(right)
    greets_below = has_below & jnp.logical_not(near_middle[0]) if relayed else has_below
    pl.when(has_above)(lambda: greet(above))
    pl.when(greets_below)(lambda: greet(below))
    peers = 2 + as_int(has_above) + as_int(has_below)
    if relayed:
        for place, partners in (
            (is_relay[0], (middle_band - 1, middle_band)),
            (is_relay[1], (middle_band - 1,)),
            (near_middle[1], (n_lat - 1,)),
        ):
            for partner in partners:
                pl.when(place)(functools.partial(greet, (partner, across)))
        peers += 2 * as_int(near_middle[0]) + as_int(is_relay[1])
    pl.semaphore_wait(barrier, peers)
    if relayed:

        @pl.when(near_middle[0])
        def _():
            for device in ((0, across), below):
                pl.semaphore_signal(ready, inc=1, device_id=device, device_id_type=MESH)

    def remote(src, dst, sems, index, device, landing=None):
        return pltpu.make_async_remote_copy(
            src_ref=src,
            dst_ref=dst,
            send_sem=sems.at[(0,) + index],
            recv_sem=sems.at[(1,) + (index if landing is None else landing)],
            device_id=device,
            device_id_type=MESH,
        )

    row_buffers = ((q_hbm, q_halo), (g_hbm, g_halo), (aug, a_halo))

    def row_copy(what, chunk, side):
        src, dst = row_buffers[what]
        rows = pl.ds(13, 3) if side == 0 else pl.ds(0, 3)
        strips = pl.ds(chunk * width, width)
        device, slot = (below, above)[side], side
        if relayed:
            turn = as_int(near_middle[side])
            hop = middle_band - 1 if side == 1 else n_lat - 1 - middle_band
            direction = 1 - 2 * side
            device = (
                lat + direction * (1 + turn * hop),
                lon + turn * (across - lon),
            )
            slot = side + direction * turn
        return remote(
            src.at[rows, strips],
            dst.at[slot, pl.ds(0, 3), strips],
            row_sems,
            (what, chunk, side),
            device,
            (what, chunk, slot),
        )

    def row_forward(what, chunk, side):
        buffer = row_buffers[what][1]
        strips = pl.ds(chunk * width, width)
        return remote(
            buffer.at[side, pl.ds(0, 3), strips],
            buffer.at[1 - side, pl.ds(0, 3), strips],
            row_sems,
            (what, chunk, 1 - side),
            (middle_band - 1 + side, across),
        )

    def await_rows(what, chunk, side):
        buffer = row_buffers[what][1]
        rows = buffer.at[side, pl.ds(0, 3), pl.ds(chunk * width, width)]
        remote(rows, rows, row_sems, (what, chunk, side), left).wait_recv()

    def forward(pieces, first=False):
        if not relayed:
            return
        for side in range(2):

            @pl.when(is_relay[side])
            def _():
                if first and side == 0:
                    pl.semaphore_wait(ready, 1)
                for what, chunk in pieces:
                    await_rows(what, chunk, side)
                    row_forward(what, chunk, side).start()

    def rim_copy(what, side):
        src = (k_hbm, v_hbm)[what]
        return remote(
            src.at[:, 7 if side == 0 else 0, pl.ds(4 if side == 0 else 0, 4)],
            rim_in.at[side, what, :, pl.ds(4 if side == 0 else 0, 4)],
            rim_sems,
            (what, side),
            right if side == 0 else left,
        )

    def back_copy(chunk, side):
        strips = pl.ds(chunk * width, width)
        return remote(
            dq_send.at[side, :, strips],
            dq_recv.at[1 - side, :, strips],
            back_sems,
            (chunk, 1 - side),
            (lat - 1 + 2 * side, lon),
        )

    def grad_copy(what, side):
        return remote(
            rim_send.at[side, what],
            rim_recv.at[side, what],
            grad_sems,
            (what, side),
            right if side == 0 else left,
        )

    has = (has_above, has_below)

    def send_rows(whats, side, chunks):
        for chunk in chunks:
            for what in whats:
                row_copy(what, chunk, side).start()

    every = range(CHUNKS)
    for side in range(2):
        if relayed:
            pl.when(near_middle[side])(functools.partial(send_rows, (0, 1), side, every))
    for chunk in every:
        for side in range(2):
            first = has[1 - side]
            if relayed:
                first = first & jnp.logical_not(near_middle[side])
            pl.when(first)(functools.partial(send_rows, (0, 1), side, (chunk,)))
    for what in range(2):
        for side in range(2):
            rim_copy(what, side).start()

    slot16 = _iota((1, 128), 1) % 16
    group16 = _iota((1, 128), 1) // 16
    low = _iota((1, 128), 1) < 64
    head_keep = [(group16 == h) | (slot16 >= 6) for h in range(8)]
    for t in range(2):
        feat[t] = _key_features(base, 8 * t, 8, base, total, 2, 0)
    feat_halo[0] = _key_features(base, 0, 4, base - 16, total, 3, 8)
    feat_halo[1] = _key_features(base, 12, 4, base + 16, total, 3, 8)

    @pl.loop(0, 9)
    def _(tile):
        dk_acc[tile] = jnp.zeros((16, 8, 512), F32)
        dv_acc[tile] = jnp.zeros((16, 8, 512), F32)

    for side in range(2):
        q_halo[side, 3] = jnp.zeros((8, 8, 512), BF)
        g_halo[side, 3] = jnp.zeros((8, 8, 512), BF)
        a_halo[side, 3] = jnp.zeros((8, 8, 128), BF)

    feature = _iota((512, 128), 0)
    lane = _iota((512, 128), 1)
    spread = jnp.where(
        (lane // 16 == feature // 64) & (lane % 16 >= 3) & (lane % 16 < 6), 1.0, 0.0
    ).astype(BF)
    for load in loads[:3]:
        load.wait()
    parts = _split3(ltv[...].T)
    column = _iota((64, 128), 0) % 8
    group = _iota((64, 128), 1) // 16
    slot = _iota((64, 128), 1) % 16
    odd = _iota((64, 128), 0) // 8 % 2
    col_hot = jnp.where((slot == 8 + odd) & (group == column), 1.0, 0.0)

    def features_of(r):
        product = _flat(gv[r].astype(F32)) * _flat(ov[r].astype(F32))
        high = product.astype(BF)
        rest = (product - high.astype(F32)).astype(BF)
        delta = _dot(high, spread, ((1,), (0,))) + _dot(rest, spread, ((1,), (0,)))
        d0, d1, d2 = _split3(delta)
        rolled = [pltpu.roll(part, (i - r) % 128, 1) for i, part in enumerate(parts)]
        value = jnp.where((slot >= 6) & (slot < 8) & (2 * group + slot - 6 == r), 1.0, col_hot)
        for i, x in enumerate(rolled + [d0, d1, d2]):
            value = jnp.where(slot == i, x, value)
        aug[r] = value.astype(BF).reshape(8, 8, 128)

    for r in (13, 14, 15):
        features_of(r)
    pl.when(has_below)(lambda: send_rows((2,), 0, every))
    for r in (0, 1, 2):
        features_of(r)
    pl.when(has_above)(lambda: send_rows((2,), 1, every))
    for r in range(3, 13):
        features_of(r)

    half = _iota((1, 8, 512), 1) < 4

    def turned(x):
        return pltpu.roll(x.astype(F32), 4, 1)

    for load in loads[3:5]:
        load.wait()

    @pl.loop(1, 8)
    def _(tile):
        for src, dst in ((kv, ksh), (vv, vsh)):
            dst[tile] = jnp.where(half, turned(src[:, tile - 1]), turned(src[:, tile])).astype(BF)

    loads[5].wait()
    prob_feat = _prob_features(128)

    def two(x):
        return jnp.concatenate([_keep(low, x), _keep(jnp.logical_not(low), x)], axis=0)

    def front(s, t, p):
        lanes = pl.ds(128 * p, 128)
        k_rows = pl.ds(8 * t, 8)
        q_rows = pl.ds(4 * t, 12)
        keys = jnp.concatenate(
            [_flat(ksh[s, k_rows, :, lanes]), _flat(ksh[s + 1, k_rows, :, lanes])], axis=0
        )
        values = jnp.concatenate(
            [_flat(vsh[s, k_rows, :, lanes]), _flat(vsh[s + 1, k_rows, :, lanes])], axis=0
        )
        q2 = two(_flat(qv[q_rows, s, :, lanes]))
        g2 = two(_flat(gv[q_rows, s, :, lanes]))
        extra = _flat(aug[q_rows, s])
        a2 = jnp.concatenate(
            [_keep(head_keep[2 * p], extra), _keep(head_keep[2 * p + 1], extra)], axis=0
        )
        scores = _dot(
            jnp.concatenate([keys, feat[t]], axis=1),
            jnp.concatenate([q2, a2], axis=1),
            ((1,), (1,)),
        )
        prob_grad = _dot(
            jnp.concatenate([values, prob_feat], axis=1),
            jnp.concatenate([g2, a2], axis=1),
            ((1,), (1,)),
        )
        return scores, prob_grad, q2, g2, keys

    def middle(scores, prob_grad, q2, g2, keys):
        weights = jnp.exp2(scores * EXP_SCALE)
        score_grad = (weights * prob_grad).astype(BF)
        turned_grad = score_grad.T
        turned_grad = jnp.concatenate([turned_grad[:96], turned_grad[96:]], axis=1)
        return weights.astype(BF), score_grad, turned_grad, q2, g2, keys

    def back(s, t, p, weights, score_grad, turned_grad, q2, g2, keys):
        lanes = pl.ds(128 * p, 128)
        k_rows = pl.ds(8 * t, 8)
        d_keys = _dot(score_grad, q2, ((1,), (0,)))
        d_values = _dot(weights, g2, ((1,), (0,)))
        d_query = _dot(turned_grad, two(keys), ((1,), (0,)))
        for acc, d in ((dk_acc, d_keys), (dv_acc, d_values)):
            acc[s, k_rows, :, lanes] += d[:64].reshape(8, 8, 128)
            acc[s + 1, k_rows, :, lanes] += d[64:].reshape(8, 8, 128)
        return d_query

    def pipelined(todo, one, two_, three, use):
        n = len(todo)
        first, second = {}, {}
        for i in range(n + LAG1 + LAG2):
            if i < n:
                first[i] = one(*todo[i])
            j = i - LAG1
            if 0 <= j < n:
                second[j] = two_(*first.pop(j))
            j = i - LAG1 - LAG2
            if 0 <= j < n:
                use(j, three(*todo[j], *second.pop(j)))

    def strips(which):
        todo = [(s, t, p) for s in which for p in range(4) for t in range(2)]
        upper = [None]

        def use(j, d_query):
            s, t, p = todo[j]
            if t == 0:
                upper[0] = d_query
                return
            lanes = pl.ds(128 * p, 128)
            dq_acc[pl.ds(0, 4), s, :, lanes] = upper[0][:32].reshape(4, 8, 128)
            dq_acc[pl.ds(4, 8), s, :, lanes] = (upper[0][32:] + d_query[:64]).reshape(8, 8, 128)
            dq_acc[pl.ds(12, 4), s, :, lanes] = d_query[64:].reshape(4, 8, 128)

        pipelined(todo, front, middle, back, use)

    strips([1, 2])
    forward(RELAY_STEPS[0], True)
    strips([3, 4])
    forward(RELAY_STEPS[1])

    for what in range(2):
        for side in range(2):
            rim_copy(what, side).wait()
    for i, (src, dst) in enumerate(((kv, ksh), (vv, vsh))):
        dst[0] = jnp.where(half, turned(rim_in[0, i]), turned(src[:, 0])).astype(BF)
        dst[8] = jnp.where(half, turned(src[:, 7]), turned(rim_in[1, i])).astype(BF)

    strips([0, 7])
    forward(RELAY_STEPS[2])

    prob_halo = _prob_features(96)

    def keys_of(ref, s, rows, lanes):
        return jnp.concatenate([_flat(ref[s + i, rows, :, lanes]) for i in range(3)], axis=0)

    def queries_of(ref, side, s, lanes):
        return jnp.concatenate([_flat(ref[side, :, s + i, :, lanes]) for i in range(2)], axis=0)

    def halo_front(s, side, p):
        lanes = pl.ds(128 * p, 128)
        rows = pl.ds(12 * side, 4)
        keys = keys_of(ksh, s, rows, lanes)
        values = keys_of(vsh, s, rows, lanes)
        q2 = two(queries_of(q_halo, side, s, lanes))
        g2 = two(queries_of(g_halo, side, s, lanes))
        extra = queries_of(a_halo, side, s, pl.ds(0, 128))
        a2 = jnp.concatenate(
            [_keep(head_keep[2 * p], extra), _keep(head_keep[2 * p + 1], extra)], axis=0
        )
        scores = _dot(
            jnp.concatenate([keys, feat_halo[side]], axis=1),
            jnp.concatenate([q2, a2], axis=1),
            ((1,), (1,)),
        )
        prob_grad = _dot(
            jnp.concatenate([values, prob_halo], axis=1),
            jnp.concatenate([g2, a2], axis=1),
            ((1,), (1,)),
        )
        return scores, prob_grad, q2, g2, keys

    def halo_middle(scores, prob_grad, q2, g2, keys):
        weights = jnp.exp2(scores * EXP_SCALE)
        score_grad = (weights * prob_grad).astype(BF)
        return weights.astype(BF), score_grad, score_grad.T, q2, g2, keys

    def halo_back(s, side, p, weights, score_grad, turned_grad, q2, g2, keys):
        lanes = pl.ds(128 * p, 128)
        rows = pl.ds(12 * side, 4)
        d_keys = _dot(score_grad, q2, ((1,), (0,)))
        d_values = _dot(weights, g2, ((1,), (0,)))
        d_query = _dot(turned_grad, keys, ((1,), (0,)))
        d_query = jnp.where(low, d_query[:64], d_query[64:]) * 0.125
        for i in range(2):
            part = d_query[32 * i : 32 * i + 24].reshape(3, 8, 128)
            dq_send[side, :, s + i, :, lanes] = part.astype(BF)
        for acc, d in ((dk_acc, d_keys), (dv_acc, d_values)):
            for i in range(3):
                acc[s + i, rows, :, lanes] += d[32 * i : 32 * i + 32].reshape(4, 8, 128)

    @pl.loop(0, 2 * CHUNKS)
    def _(k):
        chunk, side = k // 2, k % 2
        if relayed:
            middle_one = as_int(near_middle[0] | near_middle[1])
            chunk = chunk + middle_one * (k % CHUNKS - chunk)
            side = side + middle_one * (k // CHUNKS - side)
            turn = as_int(near_middle[1])
            side = side + turn * (1 - 2 * side)

        @pl.when(has_above & (side == 0) | has_below & (side == 1))
        def _():
            for what in range(3):
                await_rows(what, chunk, side)
            todo = [(chunk * width + 2 * i, side, p) for i in range(width // 2) for p in range(4)]
            pipelined(todo, halo_front, halo_middle, halo_back, lambda j, done: None)
            if relayed:

                @pl.when(near_middle[1] & (side == 0) & (chunk == 0))
                def _():
                    pl.semaphore_wait(ready, 1)

            back_copy(chunk, side).start()

    half8 = _iota((1, 8, 512), 1) < 4
    for what, acc in enumerate((dk_acc, dv_acc)):
        scale = 0.125 if what == 0 else 1.0
        for i in range(8):
            a, b = acc[8, 2 * i], acc[8, 2 * i + 1]
            rim_send[0, what, i] = (
                jnp.where(half8[0], pltpu.roll(a, 4, 0), b) * scale
            ).astype(BF)
            a, b = acc[0, 2 * i], acc[0, 2 * i + 1]
            rim_send[1, what, i] = (
                jnp.where(half8[0], a, pltpu.roll(b, 4, 0)) * scale
            ).astype(BF)
        for side in range(2):
            grad_copy(what, side).start()

    strips([5, 6])

    @pl.loop(3, 13)
    def _(r):
        dq_out[r] = (dq_acc[r] * 0.125).astype(BF)

    def merged(acc, j, scale):
        return pltpu.roll(jnp.where(half, acc[j + 1], acc[j]), 4, 1) * scale

    @pl.loop(1, 7)
    def _(j):
        dk_out[:, j] = merged(dk_acc, j, 0.125).astype(BF)
        dv_out[:, j] = merged(dv_acc, j, 1.0).astype(BF)

    for what in range(2):
        for side in range(2):
            grad_copy(what, side).wait()
    for what, (acc, out) in enumerate(((dk_acc, dk_out), (dv_acc, dv_out))):
        scale = 0.125 if what == 0 else 1.0
        edge = merged(acc, 0, scale)
        came = rim_recv[0, what].astype(F32)
        spun = pltpu.roll(came, 4, 1)
        for i in range(8):
            out[2 * i, 0] = (edge[2 * i] + _keep(half8[0], came[i])).astype(BF)
            out[2 * i + 1, 0] = (edge[2 * i + 1] + _keep(half8[0], spun[i])).astype(BF)
        edge = merged(acc, 7, scale)
        came = rim_recv[1, what].astype(F32)
        spun = pltpu.roll(came, 4, 1)
        for i in range(8):
            out[2 * i, 7] = (edge[2 * i] + _keep(jnp.logical_not(half8[0]), spun[i])).astype(BF)
            out[2 * i + 1, 7] = (
                edge[2 * i + 1] + _keep(jnp.logical_not(half8[0]), came[i])
            ).astype(BF)

    def finish(side, rows):
        @pl.when(has_above if side == 0 else has_below)
        def _():
            for chunk in range(CHUNKS):
                back_copy(chunk, 1 - side).wait_recv()
            for r in range(3):
                dq_out[rows + r] = (
                    dq_acc[rows + r] * 0.125 + dq_recv[side, r].astype(F32)
                ).astype(BF)

        @pl.when(jnp.logical_not(has_above if side == 0 else has_below))
        def _():
            for r in range(3):
                dq_out[rows + r] = (dq_acc[rows + r] * 0.125).astype(BF)

    finish(0, 0)
    finish(1, 13)

    def drain(send_side, back_side):
        for chunk in range(CHUNKS):
            for what in range(3):
                row_copy(what, chunk, send_side).wait_send()
            back_copy(chunk, back_side).wait_send()

    if relayed:
        for side in range(2):

            @pl.when(is_relay[side])
            def _():
                for pieces in RELAY_STEPS:
                    for what, chunk in pieces:
                        row_forward(what, chunk, side).wait_send()

    pl.when(has_below)(lambda: drain(0, 1))
    pl.when(has_above)(lambda: drain(1, 0))


def store_kernel(a, b, c, a_out, b_out, c_out, sem):
    copies = [
        pltpu.make_async_copy(src, dst, sem.at[i])
        for i, (src, dst) in enumerate(((a, a_out), (b, b_out), (c, c_out)))
    ]
    for copy in copies:
        copy.start()
    for copy in copies:
        copy.wait()


def solution(mesh):
    n_lat, n_lon = mesh.shape["lat"], mesh.shape["lon"]

    def per_device(query_tok, key_tok, value_tok, output_tok, grad_output, log_totals):
        def tiled(x):
            return x.reshape(16, 8, 8, 512)

        dma = pltpu.SemaphoreType.DMA
        token = (16, 8, 8, 512)
        shifted = (9, 16, 8, 512)
        outs = pl.pallas_call(
            functools.partial(kernel, n_lat, n_lon),
            out_shape=[pltpu.VMEM(token, BF)] * 3,
            in_specs=[pl.BlockSpec(memory_space=pltpu.HBM)] * 6,
            out_specs=[pl.BlockSpec(memory_space=pltpu.VMEM)] * 3,
            scratch_shapes=[
                pltpu.VMEM(token, BF),
                pltpu.VMEM(token, BF),
                pltpu.VMEM(token, BF),
                pltpu.VMEM(token, BF),
                pltpu.VMEM(token, BF),
                pltpu.VMEM((128, 64), F32),
                pltpu.VMEM((16, 8, 8, 128), BF),
                pltpu.VMEM(shifted, BF),
                pltpu.VMEM(shifted, BF),
                pltpu.VMEM(token, F32),
                pltpu.VMEM(shifted, F32),
                pltpu.VMEM(shifted, F32),
                pltpu.VMEM((2, 128, 128), BF),
                pltpu.VMEM((2, 96, 128), BF),
                pltpu.VMEM((2, 2, 16, 8, 512), BF),
                pltpu.VMEM((2, 4, 8, 8, 512), BF),
                pltpu.VMEM((2, 4, 8, 8, 512), BF),
                pltpu.VMEM((2, 4, 8, 8, 128), BF),
                pltpu.VMEM((2, 3, 8, 8, 512), BF),
                pltpu.VMEM((2, 3, 8, 8, 512), BF),
                pltpu.VMEM((2, 2, 8, 8, 512), BF),
                pltpu.VMEM((2, 2, 8, 8, 512), BF),
                dma((6,)),
                dma((2, 2, 2)),
                dma((2, 3, CHUNKS, 2)),
                dma((2, CHUNKS, 2)),
                dma((2, 2, 2)),
                pltpu.SemaphoreType.REGULAR,
            ],
            compiler_params=pltpu.CompilerParams(
                collective_id=0,
                has_side_effects=True,
                vmem_limit_bytes=56 * 1024 * 1024,
            ),
        )(
            tiled(query_tok),
            tiled(key_tok),
            tiled(value_tok),
            tiled(output_tok),
            tiled(grad_output),
            log_totals.reshape(128, 64),
        )
        outs = pl.pallas_call(
            store_kernel,
            out_shape=[jax.ShapeDtypeStruct(token, BF)] * 3,
            in_specs=[pl.BlockSpec(memory_space=pltpu.VMEM)] * 3,
            out_specs=[pl.BlockSpec(memory_space=pltpu.HBM)] * 3,
            scratch_shapes=[dma((3,))],
            compiler_params=pltpu.CompilerParams(vmem_limit_bytes=8 * 1024 * 1024),
        )(*outs)
        return tuple(x.reshape(16, 64, 512) for x in outs)

    return jax.shard_map(
        per_device,
        mesh=mesh,
        in_specs=(P("lat", "lon", None),) * 5 + (P(None, "lat", "lon"),),
        out_specs=(P("lat", "lon", None),) * 3,
        check_vma=False,
    )
```

```python
import functools

import jax
import jax.numpy as jnp
from jax import lax
from jax.experimental import pallas as pl
from jax.experimental.pallas import tpu as pltpu
from jax.sharding import PartitionSpec as P

MESH = pl.DeviceIdType.MESH
BF = jnp.bfloat16
F32 = jnp.float32
BIG = 32768.0
EXP_SCALE = 0.125 * 1.4426950408889634
CHUNKS = 2
LAG1 = 2
LAG2 = 2


def _iota(shape, dim):
    return lax.broadcasted_iota(jnp.int32, shape, dim)


def _dot(a, b, dims):
    return lax.dot_general(a, b, (dims, ((), ())), preferred_element_type=F32)


def _keep(mask, x):
    return jnp.where(mask, x, jnp.zeros_like(x))


def _flat(x):
    return x.reshape(-1, x.shape[-1])


def _key_features(base, row0, rows, q_base, total, tiles, spread):
    shape = (tiles * rows * 8, 128)
    key = _iota(shape, 0)
    lane = _iota(shape, 1)
    tile = key // (rows * 8)
    k_row = base + row0 + key // 8 % rows
    k_col = tile * 8 + key % 8
    group, slot = lane // 16, lane % 16
    q_row = q_base + 2 * group + slot - 6
    first = jnp.clip(q_row - 3, 0, total - 7)
    row_ok = (k_row >= first) & (k_row < first + 7)
    gap = k_col - 4 - group - jnp.where(slot == 9, spread, 0)
    col_ok = (gap >= -3) & (gap <= 3)
    row_slot = (slot == 6) | (slot == 7)
    bad = (row_slot & jnp.logical_not(row_ok)) | (
        ((slot == 8) | (slot == 9)) & jnp.logical_not(col_ok)
    )
    value = jnp.where(bad, -BIG, jnp.where(slot < 3, -8.0, 0.0))
    return value.astype(BF)


def _prob_features(keys):
    slot = _iota((keys, 128), 1) % 16
    return jnp.where((slot >= 3) & (slot < 6), -1.0, 0.0).astype(BF)


def _split3(x):
    a = x.astype(BF).astype(F32)
    rest = x - a
    b = rest.astype(BF).astype(F32)
    return a, b, rest - b


def kernel(
    n_lat,
    n_lon,
    q_hbm,
    k_hbm,
    v_hbm,
    o_hbm,
    g_hbm,
    lt_hbm,
    dq_out,
    dk_out,
    dv_out,
    qv,
    kv,
    vv,
    ov,
    gv,
    ltv,
    aug,
    ksh,
    vsh,
    dq_acc,
    dk_acc,
    dv_acc,
    feat,
    feat_halo,
    rim_in,
    q_halo,
    g_halo,
    a_halo,
    dq_send,
    dq_recv,
    rim_send,
    rim_recv,
    load_sem,
    rim_sems,
    row_sems,
    back_sems,
    grad_sems,
    ready,
):
    lat = lax.axis_index("lat")
    lon = lax.axis_index("lon")
    left = (lat, lax.rem(lon + n_lon - 1, n_lon))
    right = (lat, lax.rem(lon + 1, n_lon))
    above = (lat - 1, lon)
    below = (lat + 1, lon)
    has_above = lat > 0
    has_below = lat < n_lat - 1
    middle_band = n_lat // 2
    apart = n_lat >= 4
    late_peer = lat == middle_band if apart else False

    def as_int(condition):
        return jnp.where(condition, 1, 0)

    total = n_lat * 16
    base = lat * 16
    width = 8 // CHUNKS

    loads = [
        pltpu.make_async_copy(src, dst, load_sem.at[i])
        for i, (src, dst) in enumerate(
            ((g_hbm, gv), (o_hbm, ov), (lt_hbm, ltv), (k_hbm, kv), (v_hbm, vv), (q_hbm, qv))
        )
    ]
    for load in loads:
        load.start()

    barrier = pltpu.get_barrier_semaphore()

    def greet(device):
        pl.semaphore_signal(barrier, inc=1, device_id=device, device_id_type=MESH)

    greet(left)
    greet(right)
    greets_below = has_below
    if apart:
        greets_below = has_below & (lat != middle_band - 1)
    pl.when(has_above)(lambda: greet(above))
    pl.when(greets_below)(lambda: greet(below))
    peers = 2 + as_int(has_above) + as_int(has_below)
    if apart:
        peers -= as_int(late_peer)
    pl.semaphore_wait(barrier, peers)
    if apart:

        @pl.when(lat == middle_band - 1)
        def _():
            pl.semaphore_signal(ready, inc=1, device_id=below, device_id_type=MESH)

    def remote(src, dst, sems, index, device):
        return pltpu.make_async_remote_copy(
            src_ref=src,
            dst_ref=dst,
            send_sem=sems.at[(0,) + index],
            recv_sem=sems.at[(1,) + index],
            device_id=device,
            device_id_type=MESH,
        )

    row_buffers = ((q_hbm, q_halo), (g_hbm, g_halo), (aug, a_halo))

    def row_copy(what, chunk, side):
        src, dst = row_buffers[what]
        rows = pl.ds(13, 3) if side == 0 else pl.ds(0, 3)
        strips = pl.ds(chunk * width, width)
        return remote(
            src.at[rows, strips],
            dst.at[side, pl.ds(0, 3), strips],
            row_sems,
            (what, chunk, side),
            (below, above)[side],
        )

    def await_rows(what, chunk, side):
        buffer = row_buffers[what][1]
        rows = buffer.at[side, pl.ds(0, 3), pl.ds(chunk * width, width)]
        remote(rows, rows, row_sems, (what, chunk, side), left).wait_recv()

    def rim_copy(what, side):
        src = (k_hbm, v_hbm)[what]
        return remote(
            src.at[:, 7 if side == 0 else 0, pl.ds(4 if side == 0 else 0, 4)],
            rim_in.at[side, what, :, pl.ds(4 if side == 0 else 0, 4)],
            rim_sems,
            (what, side),
            right if side == 0 else left,
        )

    def back_copy(chunk, side):
        strips = pl.ds(chunk * width, width)
        return remote(
            dq_send.at[side, :, strips],
            dq_recv.at[1 - side, :, strips],
            back_sems,
            (chunk, 1 - side),
            (lat - 1 + 2 * side, lon),
        )

    def await_back(chunk, side):
        part = dq_recv.at[side, :, pl.ds(chunk * width, width)]
        remote(part, part, back_sems, (chunk, side), left).wait_recv()

    rim_parts = ((2, 4), (0, 2), (6, 2))

    def grad_copy(what, side, part):
        pairs = pl.ds(*rim_parts[part])
        return remote(
            rim_send.at[side, what, pairs],
            rim_recv.at[side, what, pairs],
            grad_sems,
            (what, side, part),
            right if side == 0 else left,
        )

    has = (has_above, has_below)

    def send_rows(whats, side, chunks):
        for chunk in chunks:
            for what in whats:
                row_copy(what, chunk, side).start()

    every = range(CHUNKS)
    if apart:
        pl.when(lat == middle_band - 1)(functools.partial(send_rows, (0, 1), 0, every))
    for chunk in every:
        for side in range(2):
            first = has[1 - side]
            if apart:
                first = first & (lat != middle_band - 1 + side)
            pl.when(first)(functools.partial(send_rows, (0, 1), side, (chunk,)))
    for what in range(2):
        for side in range(2):
            rim_copy(what, side).start()

    slot16 = _iota((1, 128), 1) % 16
    group16 = _iota((1, 128), 1) // 16
    low = _iota((1, 128), 1) < 64
    head_keep = [(group16 == h) | (slot16 >= 6) for h in range(8)]
    for t in range(2):
        feat[t] = _key_features(base, 8 * t, 8, base, total, 2, 0)
    feat_halo[0] = _key_features(base, 0, 4, base - 16, total, 3, 8)
    feat_halo[1] = _key_features(base, 12, 4, base + 16, total, 3, 8)

    @pl.loop(0, 9)
    def _(tile):
        dk_acc[tile] = jnp.zeros((16, 8, 512), F32)
        dv_acc[tile] = jnp.zeros((16, 8, 512), F32)

    for side in range(2):
        q_halo[side, 3] = jnp.zeros((8, 8, 512), BF)
        g_halo[side, 3] = jnp.zeros((8, 8, 512), BF)
        a_halo[side, 3] = jnp.zeros((8, 8, 128), BF)

    feature = _iota((512, 128), 0)
    lane = _iota((512, 128), 1)
    spread = jnp.where(
        (lane // 16 == feature // 64) & (lane % 16 >= 3) & (lane % 16 < 6), 1.0, 0.0
    ).astype(BF)
    for load in loads[:3]:
        load.wait()
    parts = _split3(ltv[...].T)
    column = _iota((64, 128), 0) % 8
    group = _iota((64, 128), 1) // 16
    slot = _iota((64, 128), 1) % 16
    odd = _iota((64, 128), 0) // 8 % 2
    col_hot = jnp.where((slot == 8 + odd) & (group == column), 1.0, 0.0)

    def features_of(r):
        product = _flat(gv[r].astype(F32)) * _flat(ov[r].astype(F32))
        high = product.astype(BF)
        rest = (product - high.astype(F32)).astype(BF)
        delta = _dot(high, spread, ((1,), (0,))) + _dot(rest, spread, ((1,), (0,)))
        d0, d1, d2 = _split3(delta)
        rolled = [pltpu.roll(part, (i - r) % 128, 1) for i, part in enumerate(parts)]
        value = jnp.where((slot >= 6) & (slot < 8) & (2 * group + slot - 6 == r), 1.0, col_hot)
        for i, x in enumerate(rolled + [d0, d1, d2]):
            value = jnp.where(slot == i, x, value)
        aug[r] = value.astype(BF).reshape(8, 8, 128)

    for r in (13, 14, 15):
        features_of(r)
    pl.when(has_below)(lambda: send_rows((2,), 0, every))
    for r in (0, 1, 2):
        features_of(r)
    early = has_above & jnp.logical_not(late_peer) if apart else has_above
    pl.when(early)(lambda: send_rows((2,), 1, every))
    for r in range(3, 13):
        features_of(r)

    half = _iota((1, 8, 512), 1) < 4

    def turned(x):
        return pltpu.roll(x.astype(F32), 4, 1)

    for load in loads[3:5]:
        load.wait()

    @pl.loop(1, 8)
    def _(tile):
        for src, dst in ((kv, ksh), (vv, vsh)):
            dst[tile] = jnp.where(half, turned(src[:, tile - 1]), turned(src[:, tile])).astype(BF)

    loads[5].wait()
    prob_feat = _prob_features(128)

    def two(x):
        return jnp.concatenate([_keep(low, x), _keep(jnp.logical_not(low), x)], axis=0)

    def front(s, t, p):
        lanes = pl.ds(128 * p, 128)
        k_rows = pl.ds(8 * t, 8)
        q_rows = pl.ds(4 * t, 12)
        keys = jnp.concatenate(
            [_flat(ksh[s, k_rows, :, lanes]), _flat(ksh[s + 1, k_rows, :, lanes])], axis=0
        )
        values = jnp.concatenate(
            [_flat(vsh[s, k_rows, :, lanes]), _flat(vsh[s + 1, k_rows, :, lanes])], axis=0
        )
        q2 = two(_flat(qv[q_rows, s, :, lanes]))
        g2 = two(_flat(gv[q_rows, s, :, lanes]))
        extra = _flat(aug[q_rows, s])
        a2 = jnp.concatenate(
            [_keep(head_keep[2 * p], extra), _keep(head_keep[2 * p + 1], extra)], axis=0
        )
        scores = _dot(
            jnp.concatenate([keys, feat[t]], axis=1),
            jnp.concatenate([q2, a2], axis=1),
            ((1,), (1,)),
        )
        prob_grad = _dot(
            jnp.concatenate([values, prob_feat], axis=1),
            jnp.concatenate([g2, a2], axis=1),
            ((1,), (1,)),
        )
        return scores, prob_grad, q2, g2, keys

    def middle(scores, prob_grad, q2, g2, keys):
        weights = jnp.exp2(scores * EXP_SCALE)
        score_grad = (weights * prob_grad).astype(BF)
        turned_grad = score_grad.T
        turned_grad = jnp.concatenate([turned_grad[:96], turned_grad[96:]], axis=1)
        return weights.astype(BF), score_grad, turned_grad, q2, g2, keys

    def back(s, t, p, weights, score_grad, turned_grad, q2, g2, keys):
        lanes = pl.ds(128 * p, 128)
        k_rows = pl.ds(8 * t, 8)
        d_keys = _dot(score_grad, q2, ((1,), (0,)))
        d_values = _dot(weights, g2, ((1,), (0,)))
        d_query = _dot(turned_grad, two(keys), ((1,), (0,)))
        for acc, d in ((dk_acc, d_keys), (dv_acc, d_values)):
            acc[s, k_rows, :, lanes] += d[:64].reshape(8, 8, 128)
            acc[s + 1, k_rows, :, lanes] += d[64:].reshape(8, 8, 128)
        return d_query

    def pipelined(todo, one, two_, three, use):
        n = len(todo)
        first, second = {}, {}
        for i in range(n + LAG1 + LAG2):
            if i < n:
                first[i] = one(*todo[i])
            j = i - LAG1
            if 0 <= j < n:
                second[j] = two_(*first.pop(j))
            j = i - LAG1 - LAG2
            if 0 <= j < n:
                use(j, three(*todo[j], *second.pop(j)))

    def strips(which):
        todo = [(s, t, p) for s in which for p in range(4) for t in range(2)]
        upper = [None]

        def use(j, d_query):
            s, t, p = todo[j]
            if t == 0:
                upper[0] = d_query
                return
            lanes = pl.ds(128 * p, 128)
            dq_acc[pl.ds(0, 4), s, :, lanes] = upper[0][:32].reshape(4, 8, 128)
            dq_acc[pl.ds(4, 8), s, :, lanes] = (upper[0][32:] + d_query[:64]).reshape(8, 8, 128)
            dq_acc[pl.ds(12, 4), s, :, lanes] = d_query[64:].reshape(4, 8, 128)

        pipelined(todo, front, middle, back, use)

    strips([1, 2])
    if apart:

        @pl.when(late_peer)
        def _():
            pl.semaphore_wait(ready, 1)
            send_rows((0, 1, 2), 1, every)

    strips([3, 4])

    for what in range(2):
        for side in range(2):
            rim_copy(what, side).wait()
    for i, (src, dst) in enumerate(((kv, ksh), (vv, vsh))):
        dst[0] = jnp.where(half, turned(rim_in[0, i]), turned(src[:, 0])).astype(BF)
        dst[8] = jnp.where(half, turned(src[:, 7]), turned(rim_in[1, i])).astype(BF)

    strips([0, 7])

    half8 = _iota((8, 512), 0) < 4

    def send_rims(parts):
        for what, acc in enumerate((dk_acc, dv_acc)):
            scale = 0.125 if what == 0 else 1.0
            for part in parts:
                start, count = rim_parts[part]
                for i in range(start, start + count):
                    a, b = acc[8, 2 * i], acc[8, 2 * i + 1]
                    rim_send[0, what, i] = (
                        jnp.where(half8, pltpu.roll(a, 4, 0), b) * scale
                    ).astype(BF)
                    a, b = acc[0, 2 * i], acc[0, 2 * i + 1]
                    rim_send[1, what, i] = (
                        jnp.where(half8, a, pltpu.roll(b, 4, 0)) * scale
                    ).astype(BF)
                for side in range(2):
                    grad_copy(what, side, part).start()

    send_rims((0,))

    prob_halo = _prob_features(96)

    def keys_of(ref, s, rows, lanes):
        return jnp.concatenate([_flat(ref[s + i, rows, :, lanes]) for i in range(3)], axis=0)

    def queries_of(ref, side, s, lanes):
        return jnp.concatenate([_flat(ref[side, :, s + i, :, lanes]) for i in range(2)], axis=0)

    def halo_front(s, side, p):
        lanes = pl.ds(128 * p, 128)
        rows = pl.ds(12 * side, 4)
        keys = keys_of(ksh, s, rows, lanes)
        values = keys_of(vsh, s, rows, lanes)
        q2 = two(queries_of(q_halo, side, s, lanes))
        g2 = two(queries_of(g_halo, side, s, lanes))
        extra = queries_of(a_halo, side, s, pl.ds(0, 128))
        a2 = jnp.concatenate(
            [_keep(head_keep[2 * p], extra), _keep(head_keep[2 * p + 1], extra)], axis=0
        )
        scores = _dot(
            jnp.concatenate([keys, feat_halo[side]], axis=1),
            jnp.concatenate([q2, a2], axis=1),
            ((1,), (1,)),
        )
        prob_grad = _dot(
            jnp.concatenate([values, prob_halo], axis=1),
            jnp.concatenate([g2, a2], axis=1),
            ((1,), (1,)),
        )
        return scores, prob_grad, q2, g2, keys

    def halo_middle(scores, prob_grad, q2, g2, keys):
        weights = jnp.exp2(scores * EXP_SCALE)
        score_grad = (weights * prob_grad).astype(BF)
        return weights.astype(BF), score_grad, score_grad.T, q2, g2, keys

    def halo_back(s, side, p, weights, score_grad, turned_grad, q2, g2, keys):
        lanes = pl.ds(128 * p, 128)
        rows = pl.ds(12 * side, 4)
        d_keys = _dot(score_grad, q2, ((1,), (0,)))
        d_values = _dot(weights, g2, ((1,), (0,)))
        d_query = _dot(turned_grad, keys, ((1,), (0,)))
        d_query = jnp.where(low, d_query[:64], d_query[64:]) * 0.125
        for i in range(2):
            part = d_query[32 * i : 32 * i + 24].reshape(3, 8, 128)
            dq_send[side, :, s + i, :, lanes] = part.astype(BF)
        for acc, d in ((dk_acc, d_keys), (dv_acc, d_values)):
            for i in range(3):
                acc[s + i, rows, :, lanes] += d[32 * i : 32 * i + 32].reshape(4, 8, 128)

    @pl.loop(0, 2 * CHUNKS)
    def _(k):
        chunk, side = k // 2, k % 2
        if apart:
            turn = as_int(late_peer)
            chunk = chunk + turn * (k % CHUNKS - chunk)
            side = side + turn * (1 - k // CHUNKS - side)

        @pl.when(has_above & (side == 0) | has_below & (side == 1))
        def _():
            for what in range(3):
                await_rows(what, chunk, side)
            todo = [(chunk * width + 2 * i, side, p) for i in range(width // 2) for p in range(4)]
            pipelined(todo, halo_front, halo_middle, halo_back, lambda j, done: None)
            back_copy(chunk, side).start()

    send_rims((1, 2))

    strips([5, 6])

    @pl.loop(3, 13)
    def _(r):
        dq_out[r] = (dq_acc[r] * 0.125).astype(BF)

    def merged(acc, j, scale):
        return pltpu.roll(jnp.where(half, acc[j + 1], acc[j]), 4, 1) * scale

    @pl.loop(1, 7)
    def _(j):
        dk_out[:, j] = merged(dk_acc, j, 0.125).astype(BF)
        dv_out[:, j] = merged(dv_acc, j, 1.0).astype(BF)

    for what in range(2):
        for side in range(2):
            for part in range(3):
                grad_copy(what, side, part).wait()
    for what, (acc, out) in enumerate(((dk_acc, dk_out), (dv_acc, dv_out))):
        scale = 0.125 if what == 0 else 1.0
        edge = merged(acc, 0, scale)
        came = rim_recv[0, what].astype(F32)
        spun = pltpu.roll(came, 4, 1)
        for i in range(8):
            out[2 * i, 0] = (edge[2 * i] + _keep(half8, came[i])).astype(BF)
            out[2 * i + 1, 0] = (edge[2 * i + 1] + _keep(half8, spun[i])).astype(BF)
        edge = merged(acc, 7, scale)
        came = rim_recv[1, what].astype(F32)
        spun = pltpu.roll(came, 4, 1)
        for i in range(8):
            out[2 * i, 7] = (edge[2 * i] + _keep(jnp.logical_not(half8), spun[i])).astype(BF)
            out[2 * i + 1, 7] = (
                edge[2 * i + 1] + _keep(jnp.logical_not(half8), came[i])
            ).astype(BF)

    def finish(side, rows):
        @pl.when(has_above if side == 0 else has_below)
        def _():
            for chunk in range(CHUNKS):
                await_back(chunk, side)
            for r in range(3):
                dq_out[rows + r] = (
                    dq_acc[rows + r] * 0.125 + dq_recv[side, r].astype(F32)
                ).astype(BF)

        @pl.when(jnp.logical_not(has_above if side == 0 else has_below))
        def _():
            for r in range(3):
                dq_out[rows + r] = (dq_acc[rows + r] * 0.125).astype(BF)

    finish(0, 0)
    finish(1, 13)

    def drain(send_side, back_side):
        for chunk in range(CHUNKS):
            for what in range(3):
                row_copy(what, chunk, send_side).wait_send()
            back_copy(chunk, back_side).wait_send()

    pl.when(has_below)(lambda: drain(0, 1))
    pl.when(has_above)(lambda: drain(1, 0))


def store_kernel(a, b, c, a_out, b_out, c_out, sem):
    copies = [
        pltpu.make_async_copy(src, dst, sem.at[i])
        for i, (src, dst) in enumerate(((a, a_out), (b, b_out), (c, c_out)))
    ]
    for copy in copies:
        copy.start()
    for copy in copies:
        copy.wait()


def solution(mesh):
    n_lat, n_lon = mesh.shape["lat"], mesh.shape["lon"]

    def per_device(query_tok, key_tok, value_tok, output_tok, grad_output, log_totals):
        def tiled(x):
            return x.reshape(16, 8, 8, 512)

        dma = pltpu.SemaphoreType.DMA
        token = (16, 8, 8, 512)
        shifted = (9, 16, 8, 512)
        outs = pl.pallas_call(
            functools.partial(kernel, n_lat, n_lon),
            out_shape=[pltpu.VMEM(token, BF)] * 3,
            in_specs=[pl.BlockSpec(memory_space=pltpu.HBM)] * 6,
            out_specs=[pl.BlockSpec(memory_space=pltpu.VMEM)] * 3,
            scratch_shapes=[
                pltpu.VMEM(token, BF),
                pltpu.VMEM(token, BF),
                pltpu.VMEM(token, BF),
                pltpu.VMEM(token, BF),
                pltpu.VMEM(token, BF),
                pltpu.VMEM((128, 64), F32),
                pltpu.VMEM((16, 8, 8, 128), BF),
                pltpu.VMEM(shifted, BF),
                pltpu.VMEM(shifted, BF),
                pltpu.VMEM(token, F32),
                pltpu.VMEM(shifted, F32),
                pltpu.VMEM(shifted, F32),
                pltpu.VMEM((2, 128, 128), BF),
                pltpu.VMEM((2, 96, 128), BF),
                pltpu.VMEM((2, 2, 16, 8, 512), BF),
                pltpu.VMEM((2, 4, 8, 8, 512), BF),
                pltpu.VMEM((2, 4, 8, 8, 512), BF),
                pltpu.VMEM((2, 4, 8, 8, 128), BF),
                pltpu.VMEM((2, 3, 8, 8, 512), BF),
                pltpu.VMEM((2, 3, 8, 8, 512), BF),
                pltpu.VMEM((2, 2, 8, 8, 512), BF),
                pltpu.VMEM((2, 2, 8, 8, 512), BF),
                dma((6,)),
                dma((2, 2, 2)),
                dma((2, 3, CHUNKS, 2)),
                dma((2, CHUNKS, 2)),
                dma((2, 2, 2, 3)),
                pltpu.SemaphoreType.REGULAR,
            ],
            compiler_params=pltpu.CompilerParams(
                collective_id=0,
                has_side_effects=True,
                vmem_limit_bytes=56 * 1024 * 1024,
            ),
        )(
            tiled(query_tok),
            tiled(key_tok),
            tiled(value_tok),
            tiled(output_tok),
            tiled(grad_output),
            log_totals.reshape(128, 64),
        )
        outs = pl.pallas_call(
            store_kernel,
            out_shape=[jax.ShapeDtypeStruct(token, BF)] * 3,
            in_specs=[pl.BlockSpec(memory_space=pltpu.VMEM)] * 3,
            out_specs=[pl.BlockSpec(memory_space=pltpu.HBM)] * 3,
            scratch_shapes=[dma((3,))],
            compiler_params=pltpu.CompilerParams(vmem_limit_bytes=8 * 1024 * 1024),
        )(*outs)
        return tuple(x.reshape(16, 64, 512) for x in outs)

    return jax.shard_map(
        per_device,
        mesh=mesh,
        in_specs=(P("lat", "lon", None),) * 5 + (P(None, "lat", "lon"),),
        out_specs=(P("lat", "lon", None),) * 3,
        check_vma=False,
    )
```

```python
import functools

import jax
import jax.numpy as jnp
from jax import lax
from jax.experimental import pallas as pl
from jax.experimental.pallas import tpu as pltpu
from jax.sharding import PartitionSpec as P

MESH = pl.DeviceIdType.MESH
BF = jnp.bfloat16
F32 = jnp.float32
BIG = 32768.0
EXP_SCALE = 0.125 * 1.4426950408889634
CHUNKS = 2
LAG1 = 2
LAG2 = 2


def _iota(shape, dim):
    return lax.broadcasted_iota(jnp.int32, shape, dim)


def _dot(a, b, dims):
    return lax.dot_general(a, b, (dims, ((), ())), preferred_element_type=F32)


def _keep(mask, x):
    return jnp.where(mask, x, jnp.zeros_like(x))


def _flat(x):
    return x.reshape(-1, x.shape[-1])


def _key_features(base, row0, rows, q_base, total, tiles, spread):
    shape = (tiles * rows * 8, 128)
    key = _iota(shape, 0)
    lane = _iota(shape, 1)
    tile = key // (rows * 8)
    k_row = base + row0 + key // 8 % rows
    k_col = tile * 8 + key % 8
    group, slot = lane // 16, lane % 16
    q_row = q_base + 2 * group + slot - 6
    first = jnp.clip(q_row - 3, 0, total - 7)
    row_ok = (k_row >= first) & (k_row < first + 7)
    gap = k_col - 4 - group - jnp.where(slot == 9, spread, 0)
    col_ok = (gap >= -3) & (gap <= 3)
    row_slot = (slot == 6) | (slot == 7)
    bad = (row_slot & jnp.logical_not(row_ok)) | (
        ((slot == 8) | (slot == 9)) & jnp.logical_not(col_ok)
    )
    value = jnp.where(bad, -BIG, jnp.where(slot < 3, -8.0, 0.0))
    return value.astype(BF)


def _prob_features(keys):
    slot = _iota((keys, 128), 1) % 16
    return jnp.where((slot >= 3) & (slot < 6), -1.0, 0.0).astype(BF)


def _split3(x):
    a = x.astype(BF).astype(F32)
    rest = x - a
    b = rest.astype(BF).astype(F32)
    return a, b, rest - b


def kernel(
    n_lat,
    n_lon,
    q_hbm,
    k_hbm,
    v_hbm,
    o_hbm,
    g_hbm,
    lt_hbm,
    dq_out,
    dk_out,
    dv_out,
    qv,
    kv,
    vv,
    ov,
    gv,
    ltv,
    aug,
    ksh,
    vsh,
    dq_acc,
    dk_acc,
    dv_acc,
    feat,
    feat_halo,
    rim_in,
    q_halo,
    g_halo,
    a_halo,
    dq_send,
    dq_recv,
    rim_send,
    rim_recv,
    load_sem,
    rim_sems,
    row_sems,
    back_sems,
    grad_sems,
    ready,
):
    lat = lax.axis_index("lat")
    lon = lax.axis_index("lon")
    left = (lat, lax.rem(lon + n_lon - 1, n_lon))
    right = (lat, lax.rem(lon + 1, n_lon))
    above = (lat - 1, lon)
    below = (lat + 1, lon)
    has_above = lat > 0
    has_below = lat < n_lat - 1
    middle_band = n_lat // 2
    apart = n_lat >= 4
    late_peer = lat == middle_band if apart else False

    def as_int(condition):
        return jnp.where(condition, 1, 0)

    total = n_lat * 16
    base = lat * 16
    width = 8 // CHUNKS

    loads = [
        pltpu.make_async_copy(src, dst, load_sem.at[i])
        for i, (src, dst) in enumerate(
            ((g_hbm, gv), (o_hbm, ov), (lt_hbm, ltv), (k_hbm, kv), (v_hbm, vv), (q_hbm, qv))
        )
    ]
    for load in loads:
        load.start()

    barrier = pltpu.get_barrier_semaphore()

    def greet(device):
        pl.semaphore_signal(barrier, inc=1, device_id=device, device_id_type=MESH)

    greet(left)
    greet(right)
    greets_below = has_below
    if apart:
        greets_below = has_below & (lat != middle_band - 1)
    pl.when(has_above)(lambda: greet(above))
    pl.when(greets_below)(lambda: greet(below))
    peers = 2 + as_int(has_above) + as_int(has_below)
    if apart:
        peers -= as_int(late_peer)
    pl.semaphore_wait(barrier, peers)
    if apart:

        @pl.when(lat == middle_band - 1)
        def _():
            pl.semaphore_signal(ready, inc=1, device_id=below, device_id_type=MESH)

    def remote(src, dst, sems, index, device):
        return pltpu.make_async_remote_copy(
            src_ref=src,
            dst_ref=dst,
            send_sem=sems.at[(0,) + index],
            recv_sem=sems.at[(1,) + index],
            device_id=device,
            device_id_type=MESH,
        )

    row_buffers = ((q_hbm, q_halo), (g_hbm, g_halo), (aug, a_halo))

    def row_copy(what, chunk, side):
        src, dst = row_buffers[what]
        rows = pl.ds(13, 3) if side == 0 else pl.ds(0, 3)
        strips = pl.ds(chunk * width, width)
        return remote(
            src.at[rows, strips],
            dst.at[side, pl.ds(0, 3), strips],
            row_sems,
            (what, chunk, side),
            (below, above)[side],
        )

    def await_rows(what, chunk, side):
        buffer = row_buffers[what][1]
        rows = buffer.at[side, pl.ds(0, 3), pl.ds(chunk * width, width)]
        remote(rows, rows, row_sems, (what, chunk, side), left).wait_recv()

    def rim_copy(what, side):
        src = (k_hbm, v_hbm)[what]
        return remote(
            src.at[:, 7 if side == 0 else 0, pl.ds(4 if side == 0 else 0, 4)],
            rim_in.at[side, what, :, pl.ds(4 if side == 0 else 0, 4)],
            rim_sems,
            (what, side),
            right if side == 0 else left,
        )

    def back_copy(chunk, side):
        strips = pl.ds(chunk * width, width)
        return remote(
            dq_send.at[side, :, strips],
            dq_recv.at[1 - side, :, strips],
            back_sems,
            (chunk, 1 - side),
            (lat - 1 + 2 * side, lon),
        )

    def await_back(chunk, side):
        part = dq_recv.at[side, :, pl.ds(chunk * width, width)]
        remote(part, part, back_sems, (chunk, side), left).wait_recv()

    rim_parts = ((2, 4), (0, 2), (6, 2))

    def grad_copy(what, side, part):
        pairs = pl.ds(*rim_parts[part])
        return remote(
            rim_send.at[side, what, pairs],
            rim_recv.at[side, what, pairs],
            grad_sems,
            (what, side, part),
            right if side == 0 else left,
        )

    has = (has_above, has_below)

    def send_rows(whats, side, chunks):
        for chunk in chunks:
            for what in whats:
                row_copy(what, chunk, side).start()

    every = range(CHUNKS)
    if apart:
        pl.when(lat == middle_band - 1)(functools.partial(send_rows, (0, 1), 0, every[:1]))
    for chunk in every:
        for side in range(2):
            first = has[1 - side]
            if apart:
                first = first & (lat != middle_band - 1 + side)
            pl.when(first)(functools.partial(send_rows, (0, 1), side, (chunk,)))
    for what in range(2):
        for side in range(2):
            rim_copy(what, side).start()

    slot16 = _iota((1, 128), 1) % 16
    group16 = _iota((1, 128), 1) // 16
    low = _iota((1, 128), 1) < 64
    head_keep = [(group16 == h) | (slot16 >= 6) for h in range(8)]
    for t in range(2):
        feat[t] = _key_features(base, 8 * t, 8, base, total, 2, 0)
    feat_halo[0] = _key_features(base, 0, 4, base - 16, total, 3, 8)
    feat_halo[1] = _key_features(base, 12, 4, base + 16, total, 3, 8)

    @pl.loop(0, 9)
    def _(tile):
        dk_acc[tile] = jnp.zeros((16, 8, 512), F32)
        dv_acc[tile] = jnp.zeros((16, 8, 512), F32)

    for side in range(2):
        q_halo[side, 3] = jnp.zeros((8, 8, 512), BF)
        g_halo[side, 3] = jnp.zeros((8, 8, 512), BF)
        a_halo[side, 3] = jnp.zeros((8, 8, 128), BF)

    feature = _iota((512, 128), 0)
    lane = _iota((512, 128), 1)
    spread = jnp.where(
        (lane // 16 == feature // 64) & (lane % 16 >= 3) & (lane % 16 < 6), 1.0, 0.0
    ).astype(BF)
    for load in loads[:3]:
        load.wait()
    parts = _split3(ltv[...].T)
    column = _iota((64, 128), 0) % 8
    group = _iota((64, 128), 1) // 16
    slot = _iota((64, 128), 1) % 16
    odd = _iota((64, 128), 0) // 8 % 2
    col_hot = jnp.where((slot == 8 + odd) & (group == column), 1.0, 0.0)

    def features_of(r):
        product = _flat(gv[r].astype(F32)) * _flat(ov[r].astype(F32))
        high = product.astype(BF)
        rest = (product - high.astype(F32)).astype(BF)
        delta = _dot(high, spread, ((1,), (0,))) + _dot(rest, spread, ((1,), (0,)))
        d0, d1, d2 = _split3(delta)
        rolled = [pltpu.roll(part, (i - r) % 128, 1) for i, part in enumerate(parts)]
        value = jnp.where((slot >= 6) & (slot < 8) & (2 * group + slot - 6 == r), 1.0, col_hot)
        for i, x in enumerate(rolled + [d0, d1, d2]):
            value = jnp.where(slot == i, x, value)
        aug[r] = value.astype(BF).reshape(8, 8, 128)

    for r in (13, 14, 15):
        features_of(r)
    pl.when(has_below)(lambda: send_rows((2,), 0, every))
    for r in (0, 1, 2):
        features_of(r)
    early = has_above & jnp.logical_not(late_peer) if apart else has_above
    pl.when(early)(lambda: send_rows((2,), 1, every))
    for r in range(3, 13):
        features_of(r)
    if apart:
        pl.when(lat == middle_band - 1)(functools.partial(send_rows, (0, 1), 0, every[1:]))

    half = _iota((1, 8, 512), 1) < 4

    def turned(x):
        return pltpu.roll(x.astype(F32), 4, 1)

    for load in loads[3:5]:
        load.wait()

    @pl.loop(1, 8)
    def _(tile):
        for src, dst in ((kv, ksh), (vv, vsh)):
            dst[tile] = jnp.where(half, turned(src[:, tile - 1]), turned(src[:, tile])).astype(BF)

    loads[5].wait()
    prob_feat = _prob_features(128)

    def two(x):
        return jnp.concatenate([_keep(low, x), _keep(jnp.logical_not(low), x)], axis=0)

    def front(s, t, p):
        lanes = pl.ds(128 * p, 128)
        k_rows = pl.ds(8 * t, 8)
        q_rows = pl.ds(4 * t, 12)
        keys = jnp.concatenate(
            [_flat(ksh[s, k_rows, :, lanes]), _flat(ksh[s + 1, k_rows, :, lanes])], axis=0
        )
        values = jnp.concatenate(
            [_flat(vsh[s, k_rows, :, lanes]), _flat(vsh[s + 1, k_rows, :, lanes])], axis=0
        )
        q2 = two(_flat(qv[q_rows, s, :, lanes]))
        g2 = two(_flat(gv[q_rows, s, :, lanes]))
        extra = _flat(aug[q_rows, s])
        a2 = jnp.concatenate(
            [_keep(head_keep[2 * p], extra), _keep(head_keep[2 * p + 1], extra)], axis=0
        )
        scores = _dot(
            jnp.concatenate([keys, feat[t]], axis=1),
            jnp.concatenate([q2, a2], axis=1),
            ((1,), (1,)),
        )
        prob_grad = _dot(
            jnp.concatenate([values, prob_feat], axis=1),
            jnp.concatenate([g2, a2], axis=1),
            ((1,), (1,)),
        )
        return scores, prob_grad, q2, g2, keys

    def middle(scores, prob_grad, q2, g2, keys):
        weights = jnp.exp2(scores * EXP_SCALE)
        score_grad = (weights * prob_grad).astype(BF)
        turned_grad = score_grad.T
        turned_grad = jnp.concatenate([turned_grad[:96], turned_grad[96:]], axis=1)
        return weights.astype(BF), score_grad, turned_grad, q2, g2, keys

    def back(s, t, p, weights, score_grad, turned_grad, q2, g2, keys):
        lanes = pl.ds(128 * p, 128)
        k_rows = pl.ds(8 * t, 8)
        d_keys = _dot(score_grad, q2, ((1,), (0,)))
        d_values = _dot(weights, g2, ((1,), (0,)))
        d_query = _dot(turned_grad, two(keys), ((1,), (0,)))
        for acc, d in ((dk_acc, d_keys), (dv_acc, d_values)):
            acc[s, k_rows, :, lanes] += d[:64].reshape(8, 8, 128)
            acc[s + 1, k_rows, :, lanes] += d[64:].reshape(8, 8, 128)
        return d_query

    def pipelined(todo, one, two_, three, use):
        n = len(todo)
        first, second = {}, {}
        for i in range(n + LAG1 + LAG2):
            if i < n:
                first[i] = one(*todo[i])
            j = i - LAG1
            if 0 <= j < n:
                second[j] = two_(*first.pop(j))
            j = i - LAG1 - LAG2
            if 0 <= j < n:
                use(j, three(*todo[j], *second.pop(j)))

    def strips(which):
        todo = [(s, t, p) for s in which for p in range(4) for t in range(2)]
        upper = [None]

        def use(j, d_query):
            s, t, p = todo[j]
            if t == 0:
                upper[0] = d_query
                return
            lanes = pl.ds(128 * p, 128)
            dq_acc[pl.ds(0, 4), s, :, lanes] = upper[0][:32].reshape(4, 8, 128)
            dq_acc[pl.ds(4, 8), s, :, lanes] = (upper[0][32:] + d_query[:64]).reshape(8, 8, 128)
            dq_acc[pl.ds(12, 4), s, :, lanes] = d_query[64:].reshape(4, 8, 128)

        pipelined(todo, front, middle, back, use)

    if apart:

        @pl.when(late_peer)
        def _():
            pl.semaphore_wait(ready, 1)
            send_rows((0, 1, 2), 1, every)

    strips([1, 2])
    strips([3, 4])

    for what in range(2):
        for side in range(2):
            rim_copy(what, side).wait()
    for i, (src, dst) in enumerate(((kv, ksh), (vv, vsh))):
        dst[0] = jnp.where(half, turned(rim_in[0, i]), turned(src[:, 0])).astype(BF)
        dst[8] = jnp.where(half, turned(src[:, 7]), turned(rim_in[1, i])).astype(BF)

    strips([0, 7])

    half8 = _iota((8, 512), 0) < 4

    def send_rims(parts):
        for what, acc in enumerate((dk_acc, dv_acc)):
            scale = 0.125 if what == 0 else 1.0
            for part in parts:
                start, count = rim_parts[part]
                for i in range(start, start + count):
                    a, b = acc[8, 2 * i], acc[8, 2 * i + 1]
                    rim_send[0, what, i] = (
                        jnp.where(half8, pltpu.roll(a, 4, 0), b) * scale
                    ).astype(BF)
                    a, b = acc[0, 2 * i], acc[0, 2 * i + 1]
                    rim_send[1, what, i] = (
                        jnp.where(half8, a, pltpu.roll(b, 4, 0)) * scale
                    ).astype(BF)
                for side in range(2):
                    grad_copy(what, side, part).start()

    send_rims((0,))

    prob_halo = _prob_features(96)

    def keys_of(ref, s, rows, lanes):
        return jnp.concatenate([_flat(ref[s + i, rows, :, lanes]) for i in range(3)], axis=0)

    def queries_of(ref, side, s, lanes):
        return jnp.concatenate([_flat(ref[side, :, s + i, :, lanes]) for i in range(2)], axis=0)

    def halo_front(s, side, p):
        lanes = pl.ds(128 * p, 128)
        rows = pl.ds(12 * side, 4)
        keys = keys_of(ksh, s, rows, lanes)
        values = keys_of(vsh, s, rows, lanes)
        q2 = two(queries_of(q_halo, side, s, lanes))
        g2 = two(queries_of(g_halo, side, s, lanes))
        extra = queries_of(a_halo, side, s, pl.ds(0, 128))
        a2 = jnp.concatenate(
            [_keep(head_keep[2 * p], extra), _keep(head_keep[2 * p + 1], extra)], axis=0
        )
        scores = _dot(
            jnp.concatenate([keys, feat_halo[side]], axis=1),
            jnp.concatenate([q2, a2], axis=1),
            ((1,), (1,)),
        )
        prob_grad = _dot(
            jnp.concatenate([values, prob_halo], axis=1),
            jnp.concatenate([g2, a2], axis=1),
            ((1,), (1,)),
        )
        return scores, prob_grad, q2, g2, keys

    def halo_middle(scores, prob_grad, q2, g2, keys):
        weights = jnp.exp2(scores * EXP_SCALE)
        score_grad = (weights * prob_grad).astype(BF)
        return weights.astype(BF), score_grad, score_grad.T, q2, g2, keys

    def halo_back(s, side, p, weights, score_grad, turned_grad, q2, g2, keys):
        lanes = pl.ds(128 * p, 128)
        rows = pl.ds(12 * side, 4)
        d_keys = _dot(score_grad, q2, ((1,), (0,)))
        d_values = _dot(weights, g2, ((1,), (0,)))
        d_query = _dot(turned_grad, keys, ((1,), (0,)))
        d_query = jnp.where(low, d_query[:64], d_query[64:]) * 0.125
        for i in range(2):
            part = d_query[32 * i : 32 * i + 24].reshape(3, 8, 128)
            dq_send[side, :, s + i, :, lanes] = part.astype(BF)
        for acc, d in ((dk_acc, d_keys), (dv_acc, d_values)):
            for i in range(3):
                acc[s + i, rows, :, lanes] += d[32 * i : 32 * i + 32].reshape(4, 8, 128)

    @pl.loop(0, 2 * CHUNKS)
    def _(k):
        chunk, side = k // 2, k % 2
        if apart:
            turn = as_int(late_peer)
            chunk = chunk + turn * (k % CHUNKS - chunk)
            side = side + turn * (1 - k // CHUNKS - side)

        @pl.when(has_above & (side == 0) | has_below & (side == 1))
        def _():
            for what in range(3):
                await_rows(what, chunk, side)
            todo = [(chunk * width + 2 * i, side, p) for i in range(width // 2) for p in range(4)]
            pipelined(todo, halo_front, halo_middle, halo_back, lambda j, done: None)
            back_copy(chunk, side).start()

    send_rims((1, 2))

    strips([5, 6])

    @pl.loop(3, 13)
    def _(r):
        dq_out[r] = (dq_acc[r] * 0.125).astype(BF)

    def merged(acc, j, scale):
        return pltpu.roll(jnp.where(half, acc[j + 1], acc[j]), 4, 1) * scale

    @pl.loop(1, 7)
    def _(j):
        dk_out[:, j] = merged(dk_acc, j, 0.125).astype(BF)
        dv_out[:, j] = merged(dv_acc, j, 1.0).astype(BF)

    for what in range(2):
        for side in range(2):
            for part in range(3):
                grad_copy(what, side, part).wait()
    for what, (acc, out) in enumerate(((dk_acc, dk_out), (dv_acc, dv_out))):
        scale = 0.125 if what == 0 else 1.0
        edge = merged(acc, 0, scale)
        came = rim_recv[0, what].astype(F32)
        spun = pltpu.roll(came, 4, 1)
        for i in range(8):
            out[2 * i, 0] = (edge[2 * i] + _keep(half8, came[i])).astype(BF)
            out[2 * i + 1, 0] = (edge[2 * i + 1] + _keep(half8, spun[i])).astype(BF)
        edge = merged(acc, 7, scale)
        came = rim_recv[1, what].astype(F32)
        spun = pltpu.roll(came, 4, 1)
        for i in range(8):
            out[2 * i, 7] = (edge[2 * i] + _keep(jnp.logical_not(half8), spun[i])).astype(BF)
            out[2 * i + 1, 7] = (
                edge[2 * i + 1] + _keep(jnp.logical_not(half8), came[i])
            ).astype(BF)

    def finish(side, rows):
        @pl.when(has_above if side == 0 else has_below)
        def _():
            for chunk in range(CHUNKS):
                await_back(chunk, side)
            for r in range(3):
                dq_out[rows + r] = (
                    dq_acc[rows + r] * 0.125 + dq_recv[side, r].astype(F32)
                ).astype(BF)

        @pl.when(jnp.logical_not(has_above if side == 0 else has_below))
        def _():
            for r in range(3):
                dq_out[rows + r] = (dq_acc[rows + r] * 0.125).astype(BF)

    finish(0, 0)
    finish(1, 13)

    def drain(send_side, back_side):
        for chunk in range(CHUNKS):
            for what in range(3):
                row_copy(what, chunk, send_side).wait_send()
            back_copy(chunk, back_side).wait_send()

    pl.when(has_below)(lambda: drain(0, 1))
    pl.when(has_above)(lambda: drain(1, 0))


def store_kernel(a, b, c, a_out, b_out, c_out, sem):
    copies = [
        pltpu.make_async_copy(src, dst, sem.at[i])
        for i, (src, dst) in enumerate(((a, a_out), (b, b_out), (c, c_out)))
    ]
    for copy in copies:
        copy.start()
    for copy in copies:
        copy.wait()


def solution(mesh):
    n_lat, n_lon = mesh.shape["lat"], mesh.shape["lon"]

    def per_device(query_tok, key_tok, value_tok, output_tok, grad_output, log_totals):
        def tiled(x):
            return x.reshape(16, 8, 8, 512)

        dma = pltpu.SemaphoreType.DMA
        token = (16, 8, 8, 512)
        shifted = (9, 16, 8, 512)
        outs = pl.pallas_call(
            functools.partial(kernel, n_lat, n_lon),
            out_shape=[pltpu.VMEM(token, BF)] * 3,
            in_specs=[pl.BlockSpec(memory_space=pltpu.HBM)] * 6,
            out_specs=[pl.BlockSpec(memory_space=pltpu.VMEM)] * 3,
            scratch_shapes=[
                pltpu.VMEM(token, BF),
                pltpu.VMEM(token, BF),
                pltpu.VMEM(token, BF),
                pltpu.VMEM(token, BF),
                pltpu.VMEM(token, BF),
                pltpu.VMEM((128, 64), F32),
                pltpu.VMEM((16, 8, 8, 128), BF),
                pltpu.VMEM(shifted, BF),
                pltpu.VMEM(shifted, BF),
                pltpu.VMEM(token, F32),
                pltpu.VMEM(shifted, F32),
                pltpu.VMEM(shifted, F32),
                pltpu.VMEM((2, 128, 128), BF),
                pltpu.VMEM((2, 96, 128), BF),
                pltpu.VMEM((2, 2, 16, 8, 512), BF),
                pltpu.VMEM((2, 4, 8, 8, 512), BF),
                pltpu.VMEM((2, 4, 8, 8, 512), BF),
                pltpu.VMEM((2, 4, 8, 8, 128), BF),
                pltpu.VMEM((2, 3, 8, 8, 512), BF),
                pltpu.VMEM((2, 3, 8, 8, 512), BF),
                pltpu.VMEM((2, 2, 8, 8, 512), BF),
                pltpu.VMEM((2, 2, 8, 8, 512), BF),
                dma((6,)),
                dma((2, 2, 2)),
                dma((2, 3, CHUNKS, 2)),
                dma((2, CHUNKS, 2)),
                dma((2, 2, 2, 3)),
                pltpu.SemaphoreType.REGULAR,
            ],
            compiler_params=pltpu.CompilerParams(
                collective_id=0,
                has_side_effects=True,
                vmem_limit_bytes=56 * 1024 * 1024,
            ),
        )(
            tiled(query_tok),
            tiled(key_tok),
            tiled(value_tok),
            tiled(output_tok),
            tiled(grad_output),
            log_totals.reshape(128, 64),
        )
        outs = pl.pallas_call(
            store_kernel,
            out_shape=[jax.ShapeDtypeStruct(token, BF)] * 3,
            in_specs=[pl.BlockSpec(memory_space=pltpu.VMEM)] * 3,
            out_specs=[pl.BlockSpec(memory_space=pltpu.HBM)] * 3,
            scratch_shapes=[dma((3,))],
            compiler_params=pltpu.CompilerParams(vmem_limit_bytes=8 * 1024 * 1024),
        )(*outs)
        return tuple(x.reshape(16, 64, 512) for x in outs)

    return jax.shard_map(
        per_device,
        mesh=mesh,
        in_specs=(P("lat", "lon", None),) * 5 + (P(None, "lat", "lon"),),
        out_specs=(P("lat", "lon", None),) * 3,
        check_vma=False,
    )
```
